32 devices in a mesh: rep: 4 (over z), exp: 8 (over y, x, core).
Axes of the slice: x: 2, y: 2, z: 4, core: 2. Of those that a mesh axis runs over, the one named last changes fastest.
Arguments:
- tokens: bfloat16 [4096, 1024], P(('rep', 'exp')), may hold values from -6 to 6
- expert_ids: int32 [4096, 2], P(('rep', 'exp')), may hold values from 0 to 7, all different within a row; in each aligned block of 128 rows (0 to 127, 128 to 255, ...) at most 64 rows name the same one
- gate_weights: float32 [4096, 2], P(('rep', 'exp')), may hold values from 0.2 to 1
- w_gate: bfloat16 [8, 1408, 1024], P('exp'), may hold values from -0.1875 to 0.1875
- w_up: bfloat16 [8, 1408, 1024], P('exp'), may hold values from -0.1875 to 0.1875
- w_down: bfloat16 [8, 1408, 1024], P('exp'), may hold values from -0.15625 to 0.15625
- grad_out: bfloat16 [4096, 1024], P(('rep', 'exp')), may hold values from -3 to 3
Outputs:
- layer_output: bfloat16 [4096, 1024], P(('rep', 'exp'))
- grad_tokens: bfloat16 [4096, 1024], P(('rep', 'exp'))
- grad_gates: float32 [4096, 2], P(('rep', 'exp'))
- grad_w_gate: bfloat16 [8, 1408, 1024], P('exp', 'rep')
- grad_w_up: bfloat16 [8, 1408, 1024], P('exp', 'rep')
- grad_w_down: bfloat16 [8, 1408, 1024], P('exp', 'rep')
The draws below stay inside these ranges and needn't reach their ends.
Inputs may be any that keep to these rules, and one draw needn't show every extreme that they name: `expert_ids`: each token names 2 different experts. In each aligned block of 128 tokens (the tokens of one device) no expert is named more than 64 times, a bound that some block reaches.
All inputs are finite; a program needn't handle non-finite values.
Results may differ from the reference program's by a relative error of at most 0.0095.
Values may be sent and summed in bfloat16 or wider, within the bound.
A program may use at most 128 MiB of HBM per device.

```python
import math
import jax
import jax.numpy as jnp
import numpy as np
from jax import lax

D = 1024
FF = 1408
TOP = 2
T_DEV = 128
EXPERTS = 8
CAP = 64
TOKENS = 4096
N_REP = 4
N_EXP = 8


def steps_of(own_key, dims, cuts, least, high):
    gain, own = 1.0, jax.random.fold_in(own_key, 6)
    for position, blocks in cuts:
        draws = jnp.exp(jax.random.uniform(jax.random.fold_in(own, position), (blocks,), jnp.float32, least / len(cuts), high / len(cuts)))
        gain = gain * jnp.repeat(draws, dims[position] // blocks).reshape([-1 if axis == position else 1 for axis in range(len(dims))])
    return gain


def shared_out(stream_key, own, number, rows, amount, top, limit, lean):
    sequence = jax.random.permutation(stream_key, amount)
    heavy_load, common = portions_of(amount, rows * top, limit, lean, True), portions_of(amount, rows * top, limit, lean, False)
    places = jnp.arange(amount)

    def named(sizes, turn):
        used = int((sizes > 0).sum())
        fixed = max(1, used // 4)
        passed = fixed + (places - fixed + turn * (used - fixed)) % max(1, amount - fixed)
        return jnp.zeros((amount,), jnp.int32).at[sequence[jnp.where(places < fixed, places, passed)]].set(jnp.asarray(sizes, jnp.int32))

    sizes = jnp.where(number % 4 == 0, named(heavy_load, number // 4), named(common, number - number // 4 - 1))
    mixed = jax.random.permutation(jax.random.fold_in(own, 3), amount)
    donor, sink = mixed[0:amount // 2 * 2:2], mixed[1:amount // 2 * 2:2]
    room = jnp.minimum(sizes[donor] - 1, limit - sizes[sink]) // 2
    room = jnp.where((donor == sequence[0]) | (sink == sequence[0]) | (sizes[sink] == 0), 0, jnp.maximum(room, 0))
    passed = jax.random.randint(jax.random.fold_in(own, 4), (amount // 2,), 0, 1 << 20) % (room + 1)
    sizes = sizes.at[donor].add(-passed).at[sink].add(passed)
    members = jnp.searchsorted(jnp.cumsum(sizes), jnp.arange(rows * top), side="right").astype(jnp.int32)
    listing = members.reshape(top, rows).T
    listing = listing[jax.random.permutation(jax.random.fold_in(own, 1), rows)]
    turn = jax.random.randint(jax.random.fold_in(own, 2), (rows, 1), 0, top)
    return jnp.take_along_axis(listing, (jnp.arange(top)[None, :] + turn) % top, axis=1)


def portions_of(amount, total, reach, lean, full):
    weights = [(1 << 20) // math.isqrt(standing ** lean) + 1 for standing in range(1, amount + 1)]
    largest = reach if full else min(reach, max(-(-total // amount), total * weights[0] // sum(weights)))
    least = 1 if total - largest >= amount - 1 else 0
    counts, spare = [largest] + [least] * (amount - 1), total - largest - least * (amount - 1)
    while spare > 0:
        movable = [i for i in range(1, amount) if counts[i] < largest] or [i for i in range(1, amount) if counts[i] < reach]
        pool, left = sum([weights[i] for i in movable]), spare
        for i in movable:
            addition = min(reach - counts[i], max(1, left * weights[i] // pool), spare)
            counts[i] = counts[i] + addition
            spare = spare - addition
    return np.array(counts)


def bell_draw(own_key, shape, spread, most, cuts=(), kind=jnp.bfloat16):
    entries = spread * jax.random.normal(own_key, shape, jnp.float32)
    if cuts:
        entries = entries * steps_of(own_key, shape, cuts, -0.22, 0.18)
    return jnp.clip(entries, -most, most).astype(kind)


def setup_inputs(seed: int = 0) -> dict:
    streams_of = jax.random.split(jax.random.key(seed), 8)
    tokens = bell_draw(streams_of[0], (TOKENS, D), 1.0, 6.0, ((0, 32),))
    expert_ids_keys = jax.random.split(jax.random.fold_in(streams_of[1], 1), TOKENS // T_DEV)
    expert_ids_turns = jax.random.permutation(jax.random.fold_in(streams_of[1], 3), TOKENS // T_DEV)
    expert_ids = jax.vmap(lambda own, number: shared_out(jax.random.fold_in(streams_of[1], 2), own, number, T_DEV, EXPERTS, TOP, CAP, 2))(expert_ids_keys, expert_ids_turns).reshape((TOKENS, TOP))
    gate_weights = jnp.clip(0.2 + 0.8 * jax.random.uniform(streams_of[2], (TOKENS, TOP), jnp.float32) ** steps_of(streams_of[2], (TOKENS, TOP), ((0, 32),), -0.2, 0.2), 0.2, 1.0)
    w_gate = bell_draw(streams_of[3], (EXPERTS, FF, D), D ** -0.5, 0.1875, ((0, 8),))
    w_up = bell_draw(streams_of[4], (EXPERTS, FF, D), D ** -0.5, 0.1875, ((0, 8),))
    w_down = bell_draw(streams_of[5], (EXPERTS, FF, D), FF ** -0.5, 0.15625, ((0, 8),))
    grad_out = bell_draw(streams_of[6], (TOKENS, D), 0.5, 3.0, ((0, 32),))
    return {"tokens": tokens, "expert_ids": expert_ids, "gate_weights": gate_weights, "w_gate": w_gate, "w_up": w_up, "w_down": w_down, "grad_out": grad_out}


def silu_parts(gate_pre):
    sigmoid_value = jax.nn.sigmoid(gate_pre)
    active = gate_pre * sigmoid_value
    slope_term = sigmoid_value * (1.0 + gate_pre * (1.0 - sigmoid_value))
    return active, slope_term


def position_of(flat_ids, experts):
    onehot = (flat_ids[:, None] == jnp.arange(experts, dtype=jnp.int32)[None, :]).astype(jnp.int32)
    before = jnp.cumsum(onehot, axis=0) - onehot
    return jnp.sum(before * onehot, axis=1).astype(jnp.int32)


def reference(tokens, expert_ids, gate_weights, w_gate, w_up, w_down, grad_out):
    experts = EXPERTS
    capacity = CAP
    peer_count = N_EXP
    replicas = N_REP
    per_replica = peer_count * T_DEV
    gate_full = w_gate.astype(jnp.float32)
    up_full = w_up.astype(jnp.float32)
    down_full = w_down.astype(jnp.float32)
    row_total = peer_count * capacity

    def one_replica(grad_sums, replica_items):
        part_tokens, part_ids, part_gates, part_grads = replica_items
        id_blocks = part_ids.reshape(peer_count, T_DEV * TOP)
        positions = jax.vmap(lambda block_ids: position_of(block_ids, experts))(id_blocks)
        sources = jnp.arange(peer_count, dtype=jnp.int32)[:, None]
        target = (id_blocks * row_total + sources * capacity + positions).reshape(-1)
        pair_tokens = jnp.repeat(part_tokens, TOP, axis=0)
        pair_gates = part_gates.reshape(-1)
        pair_grads = jnp.repeat(part_grads, TOP, axis=0).astype(jnp.float32)
        scaled_grads = (pair_gates[:, None] * pair_grads).astype(jnp.bfloat16)
        blank_rows = jnp.zeros((experts * row_total, D), jnp.bfloat16)
        rows_in = blank_rows.at[target].set(pair_tokens).reshape(experts, row_total, D).astype(jnp.float32)
        rows_grad = blank_rows.at[target].set(scaled_grads).reshape(experts, row_total, D).astype(jnp.float32)
        gate_pre = jnp.einsum("erd,efd->erf", rows_in, gate_full)
        up_pre = jnp.einsum("erd,efd->erf", rows_in, up_full)
        active, slope_term = silu_parts(gate_pre)
        hidden = (active * up_pre).astype(jnp.bfloat16).astype(jnp.float32)
        outputs = jnp.einsum("erf,efd->erd", hidden, down_full).astype(jnp.bfloat16)
        grad_hidden = jnp.einsum("erd,efd->erf", rows_grad, down_full)
        grad_gate = (grad_hidden * up_pre * slope_term).astype(jnp.bfloat16).astype(jnp.float32)
        grad_up = (grad_hidden * active).astype(jnp.bfloat16).astype(jnp.float32)
        grad_rows = (jnp.einsum("erf,efd->erd", grad_gate, gate_full) + jnp.einsum("erf,efd->erd", grad_up, up_full)).astype(jnp.bfloat16)
        pair_outputs = outputs.reshape(experts * row_total, D)[target].astype(jnp.float32)
        pair_input_grads = grad_rows.reshape(experts * row_total, D)[target].astype(jnp.float32)
        layer_output = jnp.sum((pair_gates[:, None] * pair_outputs).reshape(per_replica, TOP, D), axis=1).astype(jnp.bfloat16)
        grad_gates = jnp.sum(pair_grads * pair_outputs, axis=1).reshape(per_replica, TOP)
        grad_tokens = jnp.sum(pair_input_grads.reshape(per_replica, TOP, D), axis=1).astype(jnp.bfloat16)
        term_gate = jnp.einsum("erf,erd->efd", grad_gate, rows_in).astype(jnp.bfloat16)
        term_up = jnp.einsum("erf,erd->efd", grad_up, rows_in).astype(jnp.bfloat16)
        term_down = jnp.einsum("erf,erd->efd", hidden, rows_grad).astype(jnp.bfloat16)
        term_gate, term_up, term_down = lax.optimization_barrier((term_gate, term_up, term_down))
        grad_sums = (grad_sums[0] + term_gate.astype(jnp.float32), grad_sums[1] + term_up.astype(jnp.float32), grad_sums[2] + term_down.astype(jnp.float32))
        return grad_sums, (layer_output, grad_tokens, grad_gates)

    zero_grads = jnp.zeros((experts, FF, D), jnp.float32)
    replica_items = (tokens.reshape(replicas, per_replica, D), expert_ids.reshape(replicas, per_replica, TOP), gate_weights.reshape(replicas, per_replica, TOP), grad_out.reshape(replicas, per_replica, D))
    grad_sums, stacked = lax.scan(one_replica, (zero_grads, zero_grads, zero_grads), replica_items)
    layer_output = stacked[0].reshape(TOKENS, D)
    grad_tokens = stacked[1].reshape(TOKENS, D)
    grad_gates = stacked[2].reshape(TOKENS, TOP)
    grad_w_gate = (grad_sums[0] / replicas).astype(jnp.bfloat16)
    grad_w_up = (grad_sums[1] / replicas).astype(jnp.bfloat16)
    grad_w_down = (grad_sums[2] / replicas).astype(jnp.bfloat16)
    return (layer_output, grad_tokens, grad_gates, grad_w_gate, grad_w_up, grad_w_down)
```

```python
import functools

import jax
import jax.numpy as jnp
from jax import lax
from jax.experimental import pallas as pl
from jax.experimental.pallas import tpu as pltpu
from jax.sharding import PartitionSpec as P


def silu_parts(gate_pre):
    sigmoid_value = jax.nn.sigmoid(gate_pre)
    active = gate_pre * sigmoid_value
    slope_term = sigmoid_value * (1.0 + gate_pre * (1.0 - sigmoid_value))
    return (active, slope_term)


def place_pairs(expert_ids, experts, capacity):
    flat_ids = expert_ids.reshape(-1)
    onehot = (flat_ids[:, None] == jnp.arange(experts, dtype=jnp.int32)[None, :]).astype(jnp.int32)
    before = jnp.cumsum(onehot, axis=0) - onehot
    position = jnp.sum(before * onehot, axis=1)
    return flat_ids * capacity + position


def expert_forward(rows_in, w_gate, w_up, w_down):
    gate_pre = jnp.einsum("erd,efd->erf", rows_in, w_gate, preferred_element_type=jnp.float32)
    up_pre = jnp.einsum("erd,efd->erf", rows_in, w_up, preferred_element_type=jnp.float32)
    active, slope_term = silu_parts(gate_pre)
    hidden = (active * up_pre).astype(jnp.bfloat16)
    outputs = jnp.einsum("erf,efd->erd", hidden, w_down, preferred_element_type=jnp.float32).astype(
        jnp.bfloat16
    )
    return (up_pre, active, slope_term, hidden, outputs)


def expert_backward(rows_grad, up_pre, active, slope_term, w_gate, w_up, w_down):
    grad_hidden = jnp.einsum("erd,efd->erf", rows_grad, w_down, preferred_element_type=jnp.float32)
    grad_gate = (grad_hidden * up_pre * slope_term).astype(jnp.bfloat16)
    grad_up = (grad_hidden * active).astype(jnp.bfloat16)
    from_gate = jnp.einsum("erf,efd->erd", grad_gate, w_gate, preferred_element_type=jnp.float32)
    from_up = jnp.einsum("erf,efd->erd", grad_up, w_up, preferred_element_type=jnp.float32)
    grad_rows = (from_gate + from_up).astype(jnp.bfloat16)
    return (grad_gate, grad_up, grad_rows)


def local_general(tokens, expert_ids, gate_weights, w_gate, w_up, w_down, grad_out):
    local_tokens, model_width = tokens.shape
    top_count = expert_ids.shape[1]
    local_experts = w_gate.shape[0]
    peer_count = lax.axis_size("exp")
    replicas = lax.axis_size("rep")
    experts = local_experts * peer_count
    capacity = 2 * top_count * local_tokens // experts
    target = place_pairs(expert_ids, experts, capacity)
    pair_tokens = jnp.repeat(tokens, top_count, axis=0)
    pair_gates = gate_weights.reshape(-1)
    pair_grads = jnp.repeat(grad_out, top_count, axis=0).astype(jnp.float32)
    scaled_grads = (pair_gates[:, None] * pair_grads).astype(jnp.bfloat16)
    blank_rows = jnp.zeros((experts * capacity, model_width), jnp.bfloat16)
    token_buffer = blank_rows.at[target].set(pair_tokens).reshape(experts, capacity, model_width)
    grad_buffer = blank_rows.at[target].set(scaled_grads).reshape(experts, capacity, model_width)
    rows_in = lax.all_to_all(token_buffer, "exp", split_axis=0, concat_axis=1, tiled=True)
    up_pre, active, slope_term, hidden, outputs = expert_forward(rows_in, w_gate, w_up, w_down)
    returned = lax.all_to_all(outputs, "exp", split_axis=1, concat_axis=0, tiled=True)
    rows_grad = lax.all_to_all(grad_buffer, "exp", split_axis=0, concat_axis=1, tiled=True)
    grad_gate, grad_up, grad_rows = expert_backward(
        rows_grad, up_pre, active, slope_term, w_gate, w_up, w_down
    )
    returned_grads = lax.all_to_all(grad_rows, "exp", split_axis=1, concat_axis=0, tiled=True)
    pair_outputs = returned.reshape(experts * capacity, model_width)[target].astype(jnp.float32)
    pair_input_grads = returned_grads.reshape(experts * capacity, model_width)[target].astype(
        jnp.float32
    )
    weighted = (pair_gates[:, None] * pair_outputs).reshape(local_tokens, top_count, model_width)
    layer_output = jnp.sum(weighted, axis=1).astype(jnp.bfloat16)
    grad_gates = jnp.sum(pair_grads * pair_outputs, axis=1).reshape(local_tokens, top_count)
    grad_tokens = jnp.sum(
        pair_input_grads.reshape(local_tokens, top_count, model_width), axis=1
    ).astype(jnp.bfloat16)
    term_gate = jnp.einsum("erf,erd->fed", grad_gate, rows_in, preferred_element_type=jnp.float32)
    term_up = jnp.einsum("erf,erd->fed", grad_up, rows_in, preferred_element_type=jnp.float32)
    term_down = jnp.einsum("erf,erd->fed", hidden, rows_grad, preferred_element_type=jnp.float32)
    summed = lax.psum_scatter(
        jnp.concatenate([term_gate, term_up, term_down], axis=2).astype(jnp.bfloat16),
        "rep",
        scatter_dimension=0,
        tiled=True,
    ).astype(jnp.float32)
    summed = jnp.swapaxes(summed, 0, 1) / replicas
    grad_w_gate = summed[:, :, :model_width].astype(jnp.bfloat16)
    grad_w_up = summed[:, :, model_width : 2 * model_width].astype(jnp.bfloat16)
    grad_w_down = summed[:, :, 2 * model_width :].astype(jnp.bfloat16)
    return (layer_output, grad_tokens, grad_gates, grad_w_gate, grad_w_up, grad_w_down)


MESH = pl.DeviceIdType.MESH


def gather_kernel(reps, half, mine_ref, all_ref, here_sem, send_sem, recv_sem, zup_sem, zdown_sem, zrecv_sem):
    z = lax.axis_index("rep")
    e = lax.axis_index("exp")
    core, x, y = e % 2, (e // 2) % 2, e // 4
    sib, xn, yn = e + 1 - 2 * core, e + 2 - 4 * x, e + 4 - 8 * y
    diag = xn + yn - e
    rows = mine_ref.shape[0]
    first, second = pl.ds(0, half), pl.ds(half, rows - half)

    barrier = pltpu.get_barrier_semaphore()
    for peer in (sib, xn, yn):
        pl.semaphore_signal(barrier, inc=1, device_id={"rep": z, "exp": peer}, device_id_type=MESH)

    @pl.when(z > 0)
    def _():
        pl.semaphore_signal(barrier, inc=1, device_id={"rep": z - 1, "exp": e}, device_id_type=MESH)

    @pl.when(z < reps - 1)
    def _():
        pl.semaphore_signal(barrier, inc=1, device_id={"rep": z + 1, "exp": e}, device_id_type=MESH)

    inside = jnp.logical_and(z > 0, z < reps - 1)

    @pl.when(inside)
    def _():
        pl.semaphore_wait(barrier, 5)

    @pl.when(jnp.logical_not(inside))
    def _():
        pl.semaphore_wait(barrier, 4)

    def plane(kind, layer, source, target, peer):
        return pltpu.make_async_remote_copy(
            src_ref=source,
            dst_ref=target,
            send_sem=send_sem.at[kind, layer],
            recv_sem=recv_sem.at[kind, layer],
            device_id={"rep": z, "exp": peer},
            device_id_type=MESH,
        )

    def along(sem, layer, source, step):
        return pltpu.make_async_remote_copy(
            src_ref=source,
            dst_ref=all_ref.at[layer, e],
            send_sem=sem.at[layer],
            recv_sem=zrecv_sem.at[layer],
            device_id={"rep": z + step, "exp": e},
            device_id_type=MESH,
        )

    def same(kind, layer, owner, part, peer):
        block = all_ref.at[layer, owner] if part is None else all_ref.at[layer, owner, part]
        return plane(kind, layer, block, block, peer)

    def direct(layer, source):
        block = all_ref.at[layer, e]
        return [
            plane(0, layer, source, block, xn),
            plane(1, layer, source, block, yn),
            plane(2, layer, source, block, sib),
        ]

    def relayed(layer):
        return [
            same(3, layer, xn, first, yn),
            same(5, layer, xn, None, sib),
            same(4, layer, yn, second, xn),
            same(6, layer, yn, None, sib),
        ]

    def inject(distance, sign):
        layer = z + sign * distance
        block = all_ref.at[layer, e]
        along(zup_sem, layer, block, 0).wait_recv()
        if sign < 0:

            @pl.when(z < reps - 1)
            def _():
                along(zup_sem, layer, block, 1).start()

        else:

            @pl.when(z > 0)
            def _():
                along(zdown_sem, layer, block, -1).start()

        for copy in direct(layer, block):
            copy.start()

    def forward(layer):
        copies = relayed(layer)
        same(0, layer, xn, None, xn).wait_recv()
        copies[0].start()
        copies[1].start()
        same(1, layer, yn, None, yn).wait_recv()
        copies[2].start()
        copies[3].start()

    def finish(layer):
        same(3, layer, diag, first, yn).wait_recv()
        same(4, layer, diag, second, xn).wait_recv()
        same(7, layer, diag, None, sib).start()

    def settle(layer, source):
        for copy in direct(layer, source) + relayed(layer) + [same(7, layer, diag, None, sib)]:
            copy.wait_send()
        for kind in (2, 5, 6, 7):
            same(kind, layer, sib, None, sib).wait_recv()

    def each(distance, action):
        @pl.when(z >= distance)
        def _():
            action(-1)

        @pl.when(z < reps - distance)
        def _():
            action(1)

    here = pltpu.make_async_copy(mine_ref, all_ref.at[z, e], here_sem)
    here.start()

    @pl.when(z < reps - 1)
    def _():
        along(zup_sem, z, mine_ref, 1).start()

    @pl.when(z > 0)
    def _():
        along(zdown_sem, z, mine_ref, -1).start()

    for copy in direct(z, mine_ref):
        copy.start()
    for distance in range(1, reps + 1):
        if distance < reps:
            each(distance, lambda sign: inject(distance, sign))
        if distance == 1:
            forward(z)
        else:
            each(distance - 1, lambda sign: forward(z + sign * (distance - 1)))
        if distance == 2:
            finish(z)
        elif distance > 2:
            each(distance - 2, lambda sign: finish(z + sign * (distance - 2)))
    each(reps - 1, lambda sign: finish(z + sign * (reps - 1)))

    here.wait()
    settle(z, mine_ref)

    @pl.when(z < reps - 1)
    def _():
        along(zup_sem, z, mine_ref, 1).wait_send()

    @pl.when(z > 0)
    def _():
        along(zdown_sem, z, mine_ref, -1).wait_send()

    def drain(distance, sign):
        layer = z + sign * distance
        block = all_ref.at[layer, e]
        settle(layer, block)
        if sign < 0:

            @pl.when(z < reps - 1)
            def _():
                along(zup_sem, layer, block, 1).wait_send()

        else:

            @pl.when(z > 0)
            def _():
                along(zdown_sem, layer, block, -1).wait_send()

    for distance in range(1, reps):
        each(distance, lambda sign: drain(distance, sign))


def gather_all(mine, reps, peers):
    rows, width = mine.shape
    dma = pltpu.SemaphoreType.DMA
    return pl.pallas_call(
        functools.partial(gather_kernel, reps, rows // 16 * 8),
        out_shape=jax.ShapeDtypeStruct((reps, peers, rows, width), mine.dtype),
        in_specs=[pl.BlockSpec(memory_space=pl.ANY)],
        out_specs=pl.BlockSpec(memory_space=pl.ANY),
        scratch_shapes=[dma, dma((8, reps)), dma((8, reps)), dma((reps,)), dma((reps,)), dma((reps,))],
        compiler_params=pltpu.CompilerParams(collective_id=0, has_side_effects=True),
    )(mine)


def split_bf16(value):
    parts = []
    for _ in range(3):
        top = lax.reduce_precision(value, 8, 7)
        parts.append(top.astype(jnp.bfloat16))
        value = value - top
    return parts


def dot(a, b, a_dim, b_dim):
    return lax.dot_general(a, b, (((a_dim,), (b_dim,)), ((), ())), preferred_element_type=jnp.float32)


def local_dense(tokens, expert_ids, gate_weights, w_gate, w_up, w_down, grad_out):
    count, width = tokens.shape
    top = expert_ids.shape[1]
    peers = lax.axis_size("exp")
    reps = lax.axis_size("rep")
    rep, exp = lax.axis_index("rep"), lax.axis_index("exp")
    capacity = 2 * top * count // peers
    w_gate, w_up, w_down = w_gate[0], w_up[0], w_down[0]
    hidden_units = w_gate.shape[0]
    share = hidden_units // reps

    chosen = expert_ids[None, :, :] == jnp.arange(peers, dtype=jnp.int32)[:, None, None]
    dense_gates = jnp.sum(jnp.where(chosen, gate_weights[None], 0.0), axis=2)
    gate_rows = jnp.stack(split_bf16(dense_gates)).reshape(-1, width)
    pad = jnp.zeros((8 - gate_rows.shape[0] % 8, width), jnp.bfloat16)
    mine = jnp.concatenate([tokens, grad_out, gate_rows, pad], axis=0)
    everything = gather_all(mine, reps, peers)

    parts = everything[:, :, 2 * count : 2 * count + 3, :].astype(jnp.float32)
    gates = jnp.sum(parts, axis=2).reshape(reps, peers, peers, count)
    gates = lax.dynamic_index_in_dim(gates, exp, 2, keepdims=False).reshape(reps * peers, count)
    used = gates > 0.0
    position = jnp.cumsum(used.astype(jnp.int32), axis=1) - 1
    slots = jnp.arange(capacity, dtype=jnp.int32)[None, :, None]
    select = (used[:, None, :] & (position[:, None, :] == slots)).astype(jnp.bfloat16)
    slot_gates = jnp.sum(select.astype(jnp.float32) * gates[:, None, :], axis=2)

    def pick(lhs, rhs):
        return jnp.einsum("bst,btd->bsd", lhs, rhs, preferred_element_type=jnp.float32)

    blocks = everything.reshape(reps * peers, -1, width)
    rows_in = pick(select, blocks[:, :count]).astype(jnp.bfloat16).reshape(-1, width)
    rows_out = pick(select, blocks[:, count : 2 * count]).astype(jnp.bfloat16).astype(jnp.float32)
    rows_grad = (slot_gates[:, :, None] * rows_out).astype(jnp.bfloat16).reshape(-1, width)

    mine_count = peers * capacity
    own_in = lax.dynamic_slice_in_dim(rows_in, rep * mine_count, mine_count, 0)
    own_grad = lax.dynamic_slice_in_dim(rows_grad, rep * mine_count, mine_count, 0)

    def inner(row_in, row_grad, gate, up, down):
        gate_pre = dot(row_in, gate, 1, 1)
        up_pre = dot(row_in, up, 1, 1)
        grad_hidden = dot(row_grad, down, 1, 1)
        active, slope = silu_parts(gate_pre)
        hidden = (active * up_pre).astype(jnp.bfloat16)
        grad_gate = (grad_hidden * up_pre * slope).astype(jnp.bfloat16)
        grad_up = (grad_hidden * active).astype(jnp.bfloat16)
        return hidden, grad_gate, grad_up

    hidden, grad_gate, grad_up = inner(own_in, own_grad, w_gate, w_up, w_down)
    outputs = dot(hidden, w_down, 1, 0).astype(jnp.bfloat16)
    grad_rows = (dot(grad_gate, w_gate, 1, 0) + dot(grad_up, w_up, 1, 0)).astype(jnp.bfloat16)
    returned = lax.all_to_all(outputs, "exp", split_axis=0, concat_axis=0, tiled=True)
    returned_grads = lax.all_to_all(grad_rows, "exp", split_axis=0, concat_axis=0, tiled=True)

    part = [lax.dynamic_slice_in_dim(w, rep * share, share, 0) for w in (w_gate, w_up, w_down)]
    hidden, grad_gate, grad_up = inner(rows_in, rows_grad, *part)
    grads = [
        (dot(a, b, 0, 0) / reps).astype(jnp.bfloat16)[None]
        for a, b in ((grad_gate, rows_in), (grad_up, rows_in), (hidden, rows_grad))
    ]

    mask = dense_gates > 0.0
    before = jnp.cumsum(mask.astype(jnp.int32), axis=1) - 1
    pair_pos = jnp.sum(jnp.where(chosen, before[:, :, None], 0), axis=0)
    target = (expert_ids * capacity + pair_pos).T.reshape(-1)
    place = (target[:, None] == jnp.arange(peers * capacity, dtype=jnp.int32)[None, :]).astype(jnp.bfloat16)
    pair_outputs = dot(place, returned, 1, 0).reshape(top, count, width)
    pair_grads = dot(place, returned_grads, 1, 0).reshape(top, count, width)
    layer_output = jnp.sum(gate_weights.T[:, :, None] * pair_outputs, axis=0).astype(jnp.bfloat16)
    grad_gates = jnp.sum(grad_out.astype(jnp.float32)[None] * pair_outputs, axis=2).T
    grad_tokens = jnp.sum(pair_grads, axis=0).astype(jnp.bfloat16)
    return (layer_output, grad_tokens, grad_gates, *grads)


def solution(mesh):
    in_specs = (
        P(("rep", "exp"), None),
        P(("rep", "exp"), None),
        P(("rep", "exp"), None),
        P("exp", None, None),
        P("exp", None, None),
        P("exp", None, None),
        P(("rep", "exp"), None),
    )
    out_specs = (
        P(("rep", "exp"), None),
        P(("rep", "exp"), None),
        P(("rep", "exp"), None),
        P("exp", "rep", None),
        P("exp", "rep", None),
        P("exp", "rep", None),
    )
    local = local_dense if (mesh.shape["rep"], mesh.shape["exp"]) == (4, 8) else local_general
    return jax.shard_map(local, mesh=mesh, in_specs=in_specs, out_specs=out_specs, check_vma=False)
```

```python
import jax
import jax.numpy as jnp
from jax import lax
from jax.experimental import pallas as pl
from jax.experimental.pallas import tpu as pltpu
from jax.sharding import PartitionSpec as P


def silu_parts(gate_pre):
    sigmoid_value = jax.nn.sigmoid(gate_pre)
    active = gate_pre * sigmoid_value
    slope_term = sigmoid_value * (1.0 + gate_pre * (1.0 - sigmoid_value))
    return (active, slope_term)


def place_pairs(expert_ids, experts, capacity):
    flat_ids = expert_ids.reshape(-1)
    onehot = (flat_ids[:, None] == jnp.arange(experts, dtype=jnp.int32)[None, :]).astype(jnp.int32)
    before = jnp.cumsum(onehot, axis=0) - onehot
    position = jnp.sum(before * onehot, axis=1)
    return flat_ids * capacity + position


def expert_forward(rows_in, w_gate, w_up, w_down):
    gate_pre = jnp.einsum("erd,efd->erf", rows_in, w_gate, preferred_element_type=jnp.float32)
    up_pre = jnp.einsum("erd,efd->erf", rows_in, w_up, preferred_element_type=jnp.float32)
    active, slope_term = silu_parts(gate_pre)
    hidden = (active * up_pre).astype(jnp.bfloat16)
    outputs = jnp.einsum("erf,efd->erd", hidden, w_down, preferred_element_type=jnp.float32).astype(
        jnp.bfloat16
    )
    return (up_pre, active, slope_term, hidden, outputs)


def expert_backward(rows_grad, up_pre, active, slope_term, w_gate, w_up, w_down):
    grad_hidden = jnp.einsum("erd,efd->erf", rows_grad, w_down, preferred_element_type=jnp.float32)
    grad_gate = (grad_hidden * up_pre * slope_term).astype(jnp.bfloat16)
    grad_up = (grad_hidden * active).astype(jnp.bfloat16)
    from_gate = jnp.einsum("erf,efd->erd", grad_gate, w_gate, preferred_element_type=jnp.float32)
    from_up = jnp.einsum("erf,efd->erd", grad_up, w_up, preferred_element_type=jnp.float32)
    grad_rows = (from_gate + from_up).astype(jnp.bfloat16)
    return (grad_gate, grad_up, grad_rows)


def local_general(tokens, expert_ids, gate_weights, w_gate, w_up, w_down, grad_out):
    local_tokens, model_width = tokens.shape
    top_count = expert_ids.shape[1]
    local_experts = w_gate.shape[0]
    peer_count = lax.axis_size("exp")
    replicas = lax.axis_size("rep")
    experts = local_experts * peer_count
    capacity = 2 * top_count * local_tokens // experts
    target = place_pairs(expert_ids, experts, capacity)
    pair_tokens = jnp.repeat(tokens, top_count, axis=0)
    pair_gates = gate_weights.reshape(-1)
    pair_grads = jnp.repeat(grad_out, top_count, axis=0).astype(jnp.float32)
    scaled_grads = (pair_gates[:, None] * pair_grads).astype(jnp.bfloat16)
    blank_rows = jnp.zeros((experts * capacity, model_width), jnp.bfloat16)
    token_buffer = blank_rows.at[target].set(pair_tokens).reshape(experts, capacity, model_width)
    grad_buffer = blank_rows.at[target].set(scaled_grads).reshape(experts, capacity, model_width)
    rows_in = lax.all_to_all(token_buffer, "exp", split_axis=0, concat_axis=1, tiled=True)
    up_pre, active, slope_term, hidden, outputs = expert_forward(rows_in, w_gate, w_up, w_down)
    returned = lax.all_to_all(outputs, "exp", split_axis=1, concat_axis=0, tiled=True)
    rows_grad = lax.all_to_all(grad_buffer, "exp", split_axis=0, concat_axis=1, tiled=True)
    grad_gate, grad_up, grad_rows = expert_backward(
        rows_grad, up_pre, active, slope_term, w_gate, w_up, w_down
    )
    returned_grads = lax.all_to_all(grad_rows, "exp", split_axis=1, concat_axis=0, tiled=True)
    pair_outputs = returned.reshape(experts * capacity, model_width)[target].astype(jnp.float32)
    pair_input_grads = returned_grads.reshape(experts * capacity, model_width)[target].astype(
        jnp.float32
    )
    weighted = (pair_gates[:, None] * pair_outputs).reshape(local_tokens, top_count, model_width)
    layer_output = jnp.sum(weighted, axis=1).astype(jnp.bfloat16)
    grad_gates = jnp.sum(pair_grads * pair_outputs, axis=1).reshape(local_tokens, top_count)
    grad_tokens = jnp.sum(
        pair_input_grads.reshape(local_tokens, top_count, model_width), axis=1
    ).astype(jnp.bfloat16)
    term_gate = jnp.einsum("erf,erd->fed", grad_gate, rows_in, preferred_element_type=jnp.float32)
    term_up = jnp.einsum("erf,erd->fed", grad_up, rows_in, preferred_element_type=jnp.float32)
    term_down = jnp.einsum("erf,erd->fed", hidden, rows_grad, preferred_element_type=jnp.float32)
    summed = lax.psum_scatter(
        jnp.concatenate([term_gate, term_up, term_down], axis=2).astype(jnp.bfloat16),
        "rep",
        scatter_dimension=0,
        tiled=True,
    ).astype(jnp.float32)
    summed = jnp.swapaxes(summed, 0, 1) / replicas
    grad_w_gate = summed[:, :, :model_width].astype(jnp.bfloat16)
    grad_w_up = summed[:, :, model_width : 2 * model_width].astype(jnp.bfloat16)
    grad_w_down = summed[:, :, 2 * model_width :].astype(jnp.bfloat16)
    return (layer_output, grad_tokens, grad_gates, grad_w_gate, grad_w_up, grad_w_down)


MESH = pl.DeviceIdType.MESH
REPS = 4
PEERS = 8
EXTRA = 16


def dot(a, b, b_dim):
    return lax.dot_general(a, b, (((1,), (b_dim,)), ((), ())), preferred_element_type=jnp.float32)


def moe_kernel(
    tokens_ref, grads_ref, gate_rows_ref, target_ref, gates_ref, w_gate_hbm, w_up_hbm, w_down_hbm,
    out_ref, grad_tokens_ref, grad_gates_ref, dw_gate_ref, dw_up_ref, dw_down_ref,
    all_ref, w_gate, w_up, w_down, rows_in, rows_grad, place_ref, gate_ref, out_acc, grad_acc, leaving, returned,
    acc_gate, acc_up, acc_down,
    load_sem, weight_sem, keep_sem, send_sem, recv_sem, zup_sem, zdown_sem, zrecv_sem, back_send, back_recv,
):
    z = lax.axis_index("rep")
    e = lax.axis_index("exp")
    core, x, y = e % 2, (e // 2) % 2, e // 4
    sib, xn, yn = e + 1 - 2 * core, e + 2 - 4 * x, e + 4 - 8 * y
    diag = xn + yn - e
    count, width = tokens_ref.shape
    rows = all_ref.shape[2]
    capacity = leaving.shape[2]
    share = w_gate.shape[0] // REPS
    first, second = pl.ds(0, rows // 32 * 16), pl.ds(rows // 32 * 16, rows - rows // 32 * 16)

    side = z // 2
    near = z + side * (3 - 2 * z)
    layers = [z]
    for step in range(1, REPS):
        mirrored = step - near if step == 1 else step
        layers.append(mirrored + side * (3 - 2 * mirrored))

    mine = all_ref.at[z, e]
    loads = [
        pltpu.make_async_copy(tokens_ref, all_ref.at[z, e, pl.ds(0, count)], load_sem.at[0]),
        pltpu.make_async_copy(grads_ref, all_ref.at[z, e, pl.ds(count, count)], load_sem.at[1]),
        pltpu.make_async_copy(gate_rows_ref, all_ref.at[z, e, pl.ds(2 * count, EXTRA)], load_sem.at[2]),
    ]
    weights = [
        pltpu.make_async_copy(w_gate_hbm, w_gate, weight_sem.at[0]),
        pltpu.make_async_copy(w_up_hbm, w_up, weight_sem.at[1]),
        pltpu.make_async_copy(w_down_hbm, w_down, weight_sem.at[2]),
    ]
    for copy in loads:
        copy.start()
    for copy in weights:
        copy.start()

    barrier = pltpu.get_barrier_semaphore()
    for shift in range(1, PEERS):
        peer = (e + shift) % PEERS
        pl.semaphore_signal(barrier, inc=1, device_id={"rep": z, "exp": peer}, device_id_type=MESH)

    @pl.when(z > 0)
    def _():
        pl.semaphore_signal(barrier, inc=1, device_id={"rep": z - 1, "exp": e}, device_id_type=MESH)

    @pl.when(z < REPS - 1)
    def _():
        pl.semaphore_signal(barrier, inc=1, device_id={"rep": z + 1, "exp": e}, device_id_type=MESH)

    inside = jnp.logical_and(z > 0, z < REPS - 1)

    @pl.when(inside)
    def _():
        pl.semaphore_wait(barrier, PEERS + 1)

    @pl.when(jnp.logical_not(inside))
    def _():
        pl.semaphore_wait(barrier, PEERS)

    def plane(kind, layer, owner, part, peer):
        block = all_ref.at[layer, owner] if part is None else all_ref.at[layer, owner, part]
        return pltpu.make_async_remote_copy(
            src_ref=block,
            dst_ref=block,
            send_sem=send_sem.at[kind, layer],
            recv_sem=recv_sem.at[kind, layer],
            device_id={"rep": z, "exp": peer},
            device_id_type=MESH,
        )

    def along(sem, layer, step):
        return pltpu.make_async_remote_copy(
            src_ref=all_ref.at[layer, e],
            dst_ref=all_ref.at[layer, e],
            send_sem=sem.at[layer],
            recv_sem=zrecv_sem.at[layer],
            device_id={"rep": z + step, "exp": e},
            device_id_type=MESH,
        )

    def direct(layer):
        return [plane(0, layer, e, None, xn), plane(1, layer, e, None, yn), plane(2, layer, e, None, sib)]

    def relayed(layer):
        return [
            plane(3, layer, xn, first, yn),
            plane(5, layer, xn, None, sib),
            plane(4, layer, yn, second, xn),
            plane(6, layer, yn, None, sib),
        ]

    def pass_on(layer, action):
        @pl.when(jnp.logical_and(layer <= z, z < REPS - 1))
        def _():
            action(along(zup_sem, layer, 1))

        @pl.when(jnp.logical_and(layer >= z, z > 0))
        def _():
            action(along(zdown_sem, layer, -1))

    def inject(step):
        layer = layers[step]
        if step:
            along(zup_sem, layer, 0).wait_recv()
        pass_on(layer, lambda copy: copy.start())
        for copy in direct(layer):
            copy.start()

    def forward(step):
        layer = layers[step]
        copies = relayed(layer)
        plane(0, layer, xn, None, xn).wait_recv()
        copies[0].start()
        copies[1].start()
        plane(1, layer, yn, None, yn).wait_recv()
        copies[2].start()
        copies[3].start()

    def finish(step):
        layer = layers[step]
        plane(3, layer, diag, first, yn).wait_recv()
        plane(4, layer, diag, second, xn).wait_recv()
        plane(7, layer, diag, None, sib).start()

    def arrive(step):
        for kind in (2, 5, 6, 7):
            plane(kind, layers[step], sib, None, sib).wait_recv()

    def drain(step):
        layer = layers[step]
        for copy in direct(layer) + relayed(layer) + [plane(7, layer, diag, None, sib)]:
            copy.wait_send()
        pass_on(layer, lambda copy: copy.wait_send())

    def pick(step):
        layer = layers[step]
        lanes = pl.ds(pl.multiple_of(e * count, count), count)
        for block in range(PEERS):
            parts = all_ref[layer, block, pl.ds(2 * count, EXTRA), lanes].astype(jnp.float32)
            gate_ref[block : block + 1, :] = jnp.sum(parts, axis=0, keepdims=True)
        gates = gate_ref[...]
        used = jnp.where(gates > 0.0, 1.0, 0.0)
        earlier = lax.broadcasted_iota(jnp.int32, (count, count), 0)
        later = lax.broadcasted_iota(jnp.int32, (count, count), 1)
        before = jnp.where(earlier < later, 1.0, 0.0).astype(jnp.bfloat16)
        position = dot(used.astype(jnp.bfloat16), before, 0)
        place_ref[...] = jnp.where(gates > 0.0, position, -1.0)

        def body(block, carry):
            slot = lax.broadcasted_iota(jnp.int32, (capacity, count), 0).astype(jnp.float32)
            select = jnp.where(slot == place_ref[pl.ds(block, 1), :], 1.0, 0.0)
            slot_gates = jnp.sum(select * gate_ref[pl.ds(block, 1), :], axis=1, keepdims=True)
            select = select.astype(jnp.bfloat16)
            span = pl.ds(pl.multiple_of(block * capacity, capacity), capacity)
            rows_in[span, :] = dot(select, all_ref[layer, block, pl.ds(0, count), :], 0).astype(jnp.bfloat16)
            rows_grad[span, :] = (
                slot_gates * dot(select, all_ref[layer, block, pl.ds(count, count), :], 0)
            ).astype(jnp.bfloat16)
            return carry

        lax.fori_loop(0, PEERS, body, 0)

    def pointwise(gate_pre, up_pre, grad_hidden):
        sigmoid = 1.0 / (1.0 + jnp.exp(-gate_pre))
        active = gate_pre * sigmoid
        slope = sigmoid * (1.0 + gate_pre * (1.0 - sigmoid))
        hidden = (active * up_pre).astype(jnp.bfloat16)
        grad_gate = (grad_hidden * up_pre * slope).astype(jnp.bfloat16)
        grad_up = (grad_hidden * active).astype(jnp.bfloat16)
        return hidden, grad_gate, grad_up

    def own_rows(low, high):
        tile = rows_in.shape[0] // 2

        def body(index, carry):
            units = pl.ds(pl.multiple_of((index // 2) * share, share), share)
            span = pl.ds(pl.multiple_of((index % 2) * tile, tile), tile)
            gate, up, down = w_gate[units, :], w_up[units, :], w_down[units, :]
            row_in, row_grad = rows_in[span, :], rows_grad[span, :]
            hidden, grad_gate, grad_up = pointwise(dot(row_in, gate, 1), dot(row_in, up, 1), dot(row_grad, down, 1))
            out_acc[span, :] += dot(hidden, down, 0)
            grad_acc[span, :] += dot(grad_gate, gate, 0) + dot(grad_up, up, 0)
            return carry

        lax.fori_loop(low, high, body, 0)

    def weight_grads(start):
        units = pl.ds(pl.multiple_of(z * share, share), share)
        row_in, row_grad = rows_in[...], rows_grad[...]
        hidden, grad_gate, grad_up = pointwise(
            dot(w_gate[units, :], row_in, 1), dot(w_up[units, :], row_in, 1), dot(w_down[units, :], row_grad, 1)
        )
        for acc, lhs, rhs in ((acc_gate, grad_gate, row_in), (acc_up, grad_up, row_in), (acc_down, hidden, row_grad)):
            if start:
                acc[...] = dot(lhs, rhs, 0)
            else:
                acc[...] += dot(lhs, rhs, 0)

    def back(which, shift, source, slot, peer):
        return pltpu.make_async_remote_copy(
            src_ref=leaving.at[which, source],
            dst_ref=returned.at[which, slot],
            send_sem=back_send.at[which, shift],
            recv_sem=back_recv.at[which, shift],
            device_id={"rep": z, "exp": peer},
            device_id_type=MESH,
        )

    def keep(which):
        return pltpu.make_async_copy(leaving.at[which, e], returned.at[which, e], keep_sem.at[which])

    for copy in loads:
        copy.wait()
    inject(0)
    out_acc[...] = jnp.zeros_like(out_acc)
    grad_acc[...] = jnp.zeros_like(grad_acc)
    for copy in weights:
        copy.wait()
    inject(1)
    forward(0)
    inject(2)
    finish(0)
    forward(1)
    arrive(0)
    pick(0)
    own_rows(0, REPS)
    inject(3)
    finish(1)
    own_rows(REPS, 2 * REPS)
    for which, acc in ((0, out_acc), (1, grad_acc)):
        leaving[which] = acc[...].astype(jnp.bfloat16).reshape(leaving.shape[1:])
    for which in range(2):
        keep(which).start()
        for shift in range(1, PEERS):
            peer = (e + shift) % PEERS
            back(which, shift, peer, e, peer).start()
    forward(2)
    weight_grads(True)
    arrive(1)
    pick(1)
    weight_grads(False)
    finish(2)
    forward(3)
    arrive(2)
    pick(2)
    weight_grads(False)
    for which in range(2):
        keep(which).wait()
        for shift in range(1, PEERS):
            source = (e + PEERS - shift) % PEERS
            back(which, shift, source, source, source).wait_recv()
    outputs = returned[0].reshape(PEERS * capacity, width)
    grads = returned[1].reshape(PEERS * capacity, width)
    column = lax.broadcasted_iota(jnp.int32, (count, PEERS * capacity), 1)
    total = jnp.zeros((count, width), jnp.float32)
    grad_total = jnp.zeros((count, width), jnp.float32)
    cotangent = all_ref[z, e, pl.ds(count, count), :].astype(jnp.float32)
    for choice in range(target_ref.shape[0]):
        place = jnp.where(column == target_ref[choice], 1.0, 0.0).astype(jnp.bfloat16)
        pair = dot(place, outputs, 0)
        total += gates_ref[choice] * pair
        grad_gates_ref[choice] = jnp.sum(cotangent * pair, axis=1, keepdims=True)
        grad_total += dot(place, grads, 0)
    out_ref[...] = total.astype(jnp.bfloat16)
    grad_tokens_ref[...] = grad_total.astype(jnp.bfloat16)
    finish(3)
    arrive(3)
    pick(3)
    weight_grads(False)
    for acc, ref in ((acc_gate, dw_gate_ref), (acc_up, dw_up_ref), (acc_down, dw_down_ref)):
        ref[...] = (acc[...] * (1.0 / REPS)).astype(jnp.bfloat16)
    for step in range(REPS):
        drain(step)
    for which in range(2):
        for shift in range(1, PEERS):
            peer = (e + shift) % PEERS
            back(which, shift, peer, e, peer).wait_send()


def split_bf16(value):
    parts = []
    for _ in range(3):
        top = lax.reduce_precision(value, 8, 7)
        parts.append(top.astype(jnp.bfloat16))
        value = value - top
    return parts


def local_dense(tokens, expert_ids, gate_weights, w_gate, w_up, w_down, grad_out):
    count, width = tokens.shape
    top = expert_ids.shape[1]
    units = w_gate.shape[1]
    share = units // REPS
    capacity = 2 * top * count // PEERS

    chosen = expert_ids[None, :, :] == jnp.arange(PEERS, dtype=jnp.int32)[:, None, None]
    dense_gates = jnp.sum(jnp.where(chosen, gate_weights[None], 0.0), axis=2)
    gate_rows = jnp.stack(split_bf16(dense_gates)).reshape(-1, width)
    gate_rows = jnp.pad(gate_rows, ((0, EXTRA - gate_rows.shape[0]), (0, 0)))
    named = jnp.any(chosen, axis=2).astype(jnp.bfloat16)
    order = jnp.arange(count)
    before = jnp.dot(
        named, (order[:, None] < order[None, :]).astype(jnp.bfloat16), preferred_element_type=jnp.float32
    ).astype(jnp.int32)
    target = expert_ids * capacity + jnp.sum(jnp.where(chosen, before[:, :, None], 0), axis=0)

    dma = pltpu.SemaphoreType.DMA
    vmem = pl.BlockSpec(memory_space=pltpu.VMEM)
    anywhere = pl.BlockSpec(memory_space=pl.ANY)
    bf16, f32 = jnp.bfloat16, jnp.float32
    slots = PEERS * capacity
    out, grad_tokens, grad_gates, *grads = pl.pallas_call(
        moe_kernel,
        out_shape=[
            jax.ShapeDtypeStruct((count, width), bf16),
            jax.ShapeDtypeStruct((count, width), bf16),
            jax.ShapeDtypeStruct((top, count, 1), f32),
            *[jax.ShapeDtypeStruct((share, width), bf16)] * 3,
        ],
        in_specs=[anywhere, anywhere, anywhere, vmem, vmem, anywhere, anywhere, anywhere],
        out_specs=[vmem] * 6,
        scratch_shapes=[
            pltpu.VMEM((REPS, PEERS, 2 * count + EXTRA, width), bf16),
            *[pltpu.VMEM((units, width), bf16)] * 3,
            pltpu.VMEM((slots, width), bf16),
            pltpu.VMEM((slots, width), bf16),
            pltpu.VMEM((PEERS, count), f32),
            pltpu.VMEM((PEERS, count), f32),
            pltpu.VMEM((slots, width), f32),
            pltpu.VMEM((slots, width), f32),
            pltpu.VMEM((2, PEERS, capacity, width), bf16),
            pltpu.VMEM((2, PEERS, capacity, width), bf16),
            *[pltpu.VMEM((share, width), f32)] * 3,
            dma((3,)),
            dma((3,)),
            dma((2,)),
            dma((8, REPS)),
            dma((8, REPS)),
            dma((REPS,)),
            dma((REPS,)),
            dma((REPS,)),
            dma((2, PEERS)),
            dma((2, PEERS)),
        ],
        compiler_params=pltpu.CompilerParams(
            collective_id=0, has_side_effects=True, vmem_limit_bytes=60 * 1024 * 1024
        ),
    )(
        tokens, grad_out, gate_rows, target.T[:, :, None], gate_weights.T[:, :, None],
        w_gate[0], w_up[0], w_down[0],
    )
    return (out, grad_tokens, grad_gates[:, :, 0].T, *[grad[None] for grad in grads])


def solution(mesh):
    in_specs = (
        P(("rep", "exp"), None),
        P(("rep", "exp"), None),
        P(("rep", "exp"), None),
        P("exp", None, None),
        P("exp", None, None),
        P("exp", None, None),
        P(("rep", "exp"), None),
    )
    out_specs = (
        P(("rep", "exp"), None),
        P(("rep", "exp"), None),
        P(("rep", "exp"), None),
        P("exp", "rep", None),
        P("exp", "rep", None),
        P("exp", "rep", None),
    )
    local = local_dense if (mesh.shape["rep"], mesh.shape["exp"]) == (REPS, PEERS) else local_general
    return jax.shard_map(local, mesh=mesh, in_specs=in_specs, out_specs=out_specs, check_vma=False)
```

```python
import jax
import jax.numpy as jnp
from jax import lax
from jax.experimental import pallas as pl
from jax.experimental.pallas import tpu as pltpu
from jax.sharding import PartitionSpec as P


def silu_parts(gate_pre):
    sigmoid_value = jax.nn.sigmoid(gate_pre)
    active = gate_pre * sigmoid_value
    slope_term = sigmoid_value * (1.0 + gate_pre * (1.0 - sigmoid_value))
    return (active, slope_term)


def place_pairs(expert_ids, experts, capacity):
    flat_ids = expert_ids.reshape(-1)
    onehot = (flat_ids[:, None] == jnp.arange(experts, dtype=jnp.int32)[None, :]).astype(jnp.int32)
    before = jnp.cumsum(onehot, axis=0) - onehot
    position = jnp.sum(before * onehot, axis=1)
    return flat_ids * capacity + position


def expert_forward(rows_in, w_gate, w_up, w_down):
    gate_pre = jnp.einsum("erd,efd->erf", rows_in, w_gate, preferred_element_type=jnp.float32)
    up_pre = jnp.einsum("erd,efd->erf", rows_in, w_up, preferred_element_type=jnp.float32)
    active, slope_term = silu_parts(gate_pre)
    hidden = (active * up_pre).astype(jnp.bfloat16)
    outputs = jnp.einsum("erf,efd->erd", hidden, w_down, preferred_element_type=jnp.float32).astype(
        jnp.bfloat16
    )
    return (up_pre, active, slope_term, hidden, outputs)


def expert_backward(rows_grad, up_pre, active, slope_term, w_gate, w_up, w_down):
    grad_hidden = jnp.einsum("erd,efd->erf", rows_grad, w_down, preferred_element_type=jnp.float32)
    grad_gate = (grad_hidden * up_pre * slope_term).astype(jnp.bfloat16)
    grad_up = (grad_hidden * active).astype(jnp.bfloat16)
    from_gate = jnp.einsum("erf,efd->erd", grad_gate, w_gate, preferred_element_type=jnp.float32)
    from_up = jnp.einsum("erf,efd->erd", grad_up, w_up, preferred_element_type=jnp.float32)
    grad_rows = (from_gate + from_up).astype(jnp.bfloat16)
    return (grad_gate, grad_up, grad_rows)


def local_general(tokens, expert_ids, gate_weights, w_gate, w_up, w_down, grad_out):
    local_tokens, model_width = tokens.shape
    top_count = expert_ids.shape[1]
    local_experts = w_gate.shape[0]
    peer_count = lax.axis_size("exp")
    replicas = lax.axis_size("rep")
    experts = local_experts * peer_count
    capacity = 2 * top_count * local_tokens // experts
    target = place_pairs(expert_ids, experts, capacity)
    pair_tokens = jnp.repeat(tokens, top_count, axis=0)
    pair_gates = gate_weights.reshape(-1)
    pair_grads = jnp.repeat(grad_out, top_count, axis=0).astype(jnp.float32)
    scaled_grads = (pair_gates[:, None] * pair_grads).astype(jnp.bfloat16)
    blank_rows = jnp.zeros((experts * capacity, model_width), jnp.bfloat16)
    token_buffer = blank_rows.at[target].set(pair_tokens).reshape(experts, capacity, model_width)
    grad_buffer = blank_rows.at[target].set(scaled_grads).reshape(experts, capacity, model_width)
    rows_in = lax.all_to_all(token_buffer, "exp", split_axis=0, concat_axis=1, tiled=True)
    up_pre, active, slope_term, hidden, outputs = expert_forward(rows_in, w_gate, w_up, w_down)
    returned = lax.all_to_all(outputs, "exp", split_axis=1, concat_axis=0, tiled=True)
    rows_grad = lax.all_to_all(grad_buffer, "exp", split_axis=0, concat_axis=1, tiled=True)
    grad_gate, grad_up, grad_rows = expert_backward(
        rows_grad, up_pre, active, slope_term, w_gate, w_up, w_down
    )
    returned_grads = lax.all_to_all(grad_rows, "exp", split_axis=1, concat_axis=0, tiled=True)
    pair_outputs = returned.reshape(experts * capacity, model_width)[target].astype(jnp.float32)
    pair_input_grads = returned_grads.reshape(experts * capacity, model_width)[target].astype(
        jnp.float32
    )
    weighted = (pair_gates[:, None] * pair_outputs).reshape(local_tokens, top_count, model_width)
    layer_output = jnp.sum(weighted, axis=1).astype(jnp.bfloat16)
    grad_gates = jnp.sum(pair_grads * pair_outputs, axis=1).reshape(local_tokens, top_count)
    grad_tokens = jnp.sum(
        pair_input_grads.reshape(local_tokens, top_count, model_width), axis=1
    ).astype(jnp.bfloat16)
    term_gate = jnp.einsum("erf,erd->fed", grad_gate, rows_in, preferred_element_type=jnp.float32)
    term_up = jnp.einsum("erf,erd->fed", grad_up, rows_in, preferred_element_type=jnp.float32)
    term_down = jnp.einsum("erf,erd->fed", hidden, rows_grad, preferred_element_type=jnp.float32)
    summed = lax.psum_scatter(
        jnp.concatenate([term_gate, term_up, term_down], axis=2).astype(jnp.bfloat16),
        "rep",
        scatter_dimension=0,
        tiled=True,
    ).astype(jnp.float32)
    summed = jnp.swapaxes(summed, 0, 1) / replicas
    grad_w_gate = summed[:, :, :model_width].astype(jnp.bfloat16)
    grad_w_up = summed[:, :, model_width : 2 * model_width].astype(jnp.bfloat16)
    grad_w_down = summed[:, :, 2 * model_width :].astype(jnp.bfloat16)
    return (layer_output, grad_tokens, grad_gates, grad_w_gate, grad_w_up, grad_w_down)


MESH = pl.DeviceIdType.MESH
REPS = 4
PEERS = 8
EXTRA = 16
RIDING = 96


def dot(a, b, b_dim):
    return lax.dot_general(a, b, (((1,), (b_dim,)), ((), ())), preferred_element_type=jnp.float32)


def moe_kernel(
    tokens_ref, grads_ref, ids_ref, gates_ref, w_gate_hbm, w_up_hbm, w_down_hbm,
    out_ref, grad_tokens_ref, grad_gates_ref, dw_gate_ref, dw_up_ref, dw_down_ref,
    all_ref, w_gate, w_up, w_down, rows_in, rows_grad, place_ref, gate_ref, out_acc, grad_acc, leaving, returned,
    acc_gate, acc_up, acc_down,
    load_sem, weight_sem, keep_sem, send_sem, recv_sem, zup_sem, zdown_sem, zrecv_sem,
    xup_sem, xdown_sem, xrecv_sem, back_send, back_recv,
):
    z = lax.axis_index("rep")
    e = lax.axis_index("exp")
    core, x, y = e % 2, (e // 2) % 2, e // 4
    sib, xn, yn = e + 1 - 2 * core, e + 2 - 4 * x, e + 4 - 8 * y
    diag = xn + yn - e
    count, width = tokens_ref.shape
    rows = all_ref.shape[2]
    capacity = leaving.shape[2]
    share = w_gate.shape[0] // REPS
    top = ids_ref.shape[1]
    cut = rows - RIDING
    riding = pl.ds(cut, RIDING)

    side = z // 2
    near = z + side * (3 - 2 * z)
    layers = [z]
    for step in range(1, REPS):
        mirrored = step - near if step == 1 else step
        layers.append(mirrored + side * (3 - 2 * mirrored))

    loads = [
        pltpu.make_async_copy(tokens_ref, all_ref.at[z, e, pl.ds(0, count)], load_sem.at[0]),
        pltpu.make_async_copy(grads_ref, all_ref.at[z, e, pl.ds(count, count)], load_sem.at[1]),
    ]
    weights = [
        pltpu.make_async_copy(w_gate_hbm, w_gate, weight_sem.at[0]),
        pltpu.make_async_copy(w_up_hbm, w_up, weight_sem.at[1]),
        pltpu.make_async_copy(w_down_hbm, w_down, weight_sem.at[2]),
    ]
    def pack_gates():
        lane = lax.broadcasted_iota(jnp.int32, (count, count), 1)
        dense = jnp.zeros((count, count), jnp.float32)
        for choice in range(top):
            dense += jnp.where(lane == ids_ref[:, choice : choice + 1], gates_ref[:, choice : choice + 1], 0.0)
        value = dense.T[:PEERS, :]
        parts = []
        for _ in range(3):
            part = value.astype(jnp.bfloat16).astype(jnp.float32)
            parts.append(part)
            value = value - part
        row = lax.broadcasted_iota(jnp.int32, (EXTRA, count), 0)
        for expert in range(PEERS):
            tile = jnp.zeros((EXTRA, count), jnp.float32)
            for index, part in enumerate(parts):
                tile = jnp.where(row == index, part[expert : expert + 1, :], tile)
            lanes = pl.ds(expert * count, count)
            all_ref[z, e, pl.ds(2 * count, EXTRA), lanes] = tile.astype(jnp.bfloat16)

    def targets():
        lane = lax.broadcasted_iota(jnp.int32, (count, count), 1)
        row = lax.broadcasted_iota(jnp.int32, (count, count), 0)
        picks = [lane == ids_ref[:, choice : choice + 1] for choice in range(top)]
        named = sum(jnp.where(picked, 1.0, 0.0) for picked in picks)
        before = dot(jnp.where(lane < row, 1.0, 0.0).astype(jnp.bfloat16), named.astype(jnp.bfloat16), 0)
        slot = before + (lane * capacity).astype(jnp.float32)
        return [jnp.sum(jnp.where(picked, slot, 0.0), axis=1, keepdims=True) for picked in picks]

    for copy in loads:
        copy.start()
    for copy in weights:
        copy.start()

    barrier = pltpu.get_barrier_semaphore()
    for shift in range(1, PEERS):
        peer = (e + shift) % PEERS
        pl.semaphore_signal(barrier, inc=1, device_id={"rep": z, "exp": peer}, device_id_type=MESH)

    @pl.when(z > 0)
    def _():
        pl.semaphore_signal(barrier, inc=1, device_id={"rep": z - 1, "exp": e}, device_id_type=MESH)

    @pl.when(z < REPS - 1)
    def _():
        pl.semaphore_signal(barrier, inc=1, device_id={"rep": z + 1, "exp": e}, device_id_type=MESH)

    pack_gates()
    inside = jnp.logical_and(z > 0, z < REPS - 1)

    @pl.when(inside)
    def _():
        pl.semaphore_wait(barrier, PEERS + 1)

    @pl.when(jnp.logical_not(inside))
    def _():
        pl.semaphore_wait(barrier, PEERS)

    def plane(kind, layer, owner, part, peer):
        block = all_ref.at[layer, owner] if part is None else all_ref.at[layer, owner, part]
        return pltpu.make_async_remote_copy(
            src_ref=block,
            dst_ref=block,
            send_sem=send_sem.at[kind, layer],
            recv_sem=recv_sem.at[kind, layer],
            device_id={"rep": z, "exp": peer},
            device_id_type=MESH,
        )

    def along(sem, layer, step):
        return pltpu.make_async_remote_copy(
            src_ref=all_ref.at[layer, e],
            dst_ref=all_ref.at[layer, e],
            send_sem=sem.at[layer],
            recv_sem=zrecv_sem.at[layer],
            device_id={"rep": z + step, "exp": e},
            device_id_type=MESH,
        )

    def spans(step):
        whole = rows if step == 0 else cut
        half = whole // 32 * 16
        return pl.ds(0, whole), pl.ds(0, half), pl.ds(half, whole - half)

    def direct(step):
        layer, (whole, _, _) = layers[step], spans(step)
        return [plane(0, layer, e, whole, xn), plane(1, layer, e, whole, yn), plane(2, layer, e, None, sib)]

    def relayed(step):
        layer, (_, first, second) = layers[step], spans(step)
        return [
            plane(3, layer, xn, first, yn),
            plane(5, layer, xn, None, sib),
            plane(4, layer, yn, second, xn),
            plane(6, layer, yn, None, sib),
        ]

    def pass_on(layer, action):
        @pl.when(jnp.logical_and(layer <= z, z < REPS - 1))
        def _():
            action(along(zup_sem, layer, 1))

        @pl.when(jnp.logical_and(layer >= z, z > 0))
        def _():
            action(along(zdown_sem, layer, -1))

    def rider(sem, index, layer, step):
        block = all_ref.at[layer, (xn, yn, diag)[index], riding]
        return pltpu.make_async_remote_copy(
            src_ref=block,
            dst_ref=block,
            send_sem=sem.at[index, layer],
            recv_sem=xrecv_sem.at[index, layer],
            device_id={"rep": z + step, "exp": e},
            device_id_type=MESH,
        )

    def pass_rider(index, layer, action):
        @pl.when(jnp.logical_and(layer <= z, z < REPS - 1))
        def _():
            action(rider(xup_sem, index, layer, 1))

        @pl.when(jnp.logical_and(layer >= z, z > 0))
        def _():
            action(rider(xdown_sem, index, layer, -1))

    def ride(step, index):
        layer = layers[step]
        if step:
            rider(xup_sem, index, layer, 0).wait_recv()
        pass_rider(index, layer, lambda copy: copy.start())

    def inject(step):
        layer = layers[step]
        if step:
            along(zup_sem, layer, 0).wait_recv()
        pass_on(layer, lambda copy: copy.start())
        for copy in direct(step):
            copy.start()

    def forward(step):
        layer, (whole, _, _) = layers[step], spans(step)
        copies = relayed(step)
        plane(0, layer, xn, whole, xn).wait_recv()
        copies[0].start()
        plane(1, layer, yn, whole, yn).wait_recv()
        copies[2].start()
        ride(step, 0)
        copies[1].start()
        ride(step, 1)
        copies[3].start()

    def finish(step):
        layer, (_, first, second) = layers[step], spans(step)
        plane(3, layer, diag, first, yn).wait_recv()
        plane(4, layer, diag, second, xn).wait_recv()
        ride(step, 2)
        plane(7, layer, diag, None, sib).start()

    def arrive(step):
        for kind in (2, 5, 6, 7):
            plane(kind, layers[step], sib, None, sib).wait_recv()

    def drain(step):
        layer = layers[step]
        for copy in direct(step) + relayed(step) + [plane(7, layer, diag, None, sib)]:
            copy.wait_send()
        pass_on(layer, lambda copy: copy.wait_send())
        for index in range(3):
            pass_rider(index, layer, lambda copy: copy.wait_send())

    def pick(step):
        layer = layers[step]
        lanes = pl.ds(pl.multiple_of(e * count, count), count)
        for block in range(PEERS):
            parts = all_ref[layer, block, pl.ds(2 * count, EXTRA), lanes].astype(jnp.float32)
            gate_ref[block : block + 1, :] = jnp.sum(parts, axis=0, keepdims=True)
        gates = gate_ref[...]
        used = jnp.where(gates > 0.0, 1.0, 0.0)
        earlier = lax.broadcasted_iota(jnp.int32, (count, count), 0)
        later = lax.broadcasted_iota(jnp.int32, (count, count), 1)
        before = jnp.where(earlier < later, 1.0, 0.0).astype(jnp.bfloat16)
        position = dot(used.astype(jnp.bfloat16), before, 0)
        place_ref[...] = jnp.where(gates > 0.0, position, -1.0)

        def body(block, carry):
            slot = lax.broadcasted_iota(jnp.int32, (capacity, count), 0).astype(jnp.float32)
            select = jnp.where(slot == place_ref[pl.ds(block, 1), :], 1.0, 0.0)
            slot_gates = jnp.sum(select * gate_ref[pl.ds(block, 1), :], axis=1, keepdims=True)
            select = select.astype(jnp.bfloat16)
            span = pl.ds(pl.multiple_of(block * capacity, capacity), capacity)
            rows_in[span, :] = dot(select, all_ref[layer, block, pl.ds(0, count), :], 0).astype(jnp.bfloat16)
            rows_grad[span, :] = (
                slot_gates * dot(select, all_ref[layer, block, pl.ds(count, count), :], 0)
            ).astype(jnp.bfloat16)
            return carry

        lax.fori_loop(0, PEERS, body, 0)

    def pointwise(gate_pre, up_pre, grad_hidden):
        sigmoid = 1.0 / (1.0 + jnp.exp(-gate_pre))
        active = gate_pre * sigmoid
        slope = sigmoid * (1.0 + gate_pre * (1.0 - sigmoid))
        hidden = (active * up_pre).astype(jnp.bfloat16)
        grad_gate = (grad_hidden * up_pre * slope).astype(jnp.bfloat16)
        grad_up = (grad_hidden * active).astype(jnp.bfloat16)
        return hidden, grad_gate, grad_up

    def own_rows(low, high):
        tile = rows_in.shape[0] // 2

        def body(index, carry):
            units = pl.ds(pl.multiple_of((index // 2) * share, share), share)
            span = pl.ds(pl.multiple_of((index % 2) * tile, tile), tile)
            gate, up, down = w_gate[units, :], w_up[units, :], w_down[units, :]
            row_in, row_grad = rows_in[span, :], rows_grad[span, :]
            hidden, grad_gate, grad_up = pointwise(dot(row_in, gate, 1), dot(row_in, up, 1), dot(row_grad, down, 1))
            out_acc[span, :] += dot(hidden, down, 0)
            grad_acc[span, :] += dot(grad_gate, gate, 0) + dot(grad_up, up, 0)
            return carry

        lax.fori_loop(low, high, body, 0)

    def weight_grads(start):
        units = pl.ds(pl.multiple_of(z * share, share), share)
        row_in, row_grad = rows_in[...], rows_grad[...]
        hidden, grad_gate, grad_up = pointwise(
            dot(w_gate[units, :], row_in, 1), dot(w_up[units, :], row_in, 1), dot(w_down[units, :], row_grad, 1)
        )
        for acc, lhs, rhs in ((acc_gate, grad_gate, row_in), (acc_up, grad_up, row_in), (acc_down, hidden, row_grad)):
            if start:
                acc[...] = dot(lhs, rhs, 0)
            else:
                acc[...] += dot(lhs, rhs, 0)

    def back(which, shift, source, slot, peer):
        return pltpu.make_async_remote_copy(
            src_ref=leaving.at[which, source],
            dst_ref=returned.at[which, slot],
            send_sem=back_send.at[which, shift],
            recv_sem=back_recv.at[which, shift],
            device_id={"rep": z, "exp": peer},
            device_id_type=MESH,
        )

    def keep(which):
        return pltpu.make_async_copy(leaving.at[which, e], returned.at[which, e], keep_sem.at[which])

    for copy in loads:
        copy.wait()
    inject(0)
    out_acc[...] = jnp.zeros_like(out_acc)
    grad_acc[...] = jnp.zeros_like(grad_acc)
    for copy in weights:
        copy.wait()
    inject(1)
    forward(0)
    inject(2)
    finish(0)
    forward(1)
    arrive(0)
    pick(0)
    own_rows(0, REPS)
    inject(3)
    finish(1)
    own_rows(REPS, 2 * REPS)
    for which, acc in ((0, out_acc), (1, grad_acc)):
        leaving[which] = acc[...].astype(jnp.bfloat16).reshape(leaving.shape[1:])
    for which in range(2):
        keep(which).start()
        for shift in range(1, PEERS):
            peer = (e + shift) % PEERS
            back(which, shift, peer, e, peer).start()
    forward(2)
    weight_grads(True)
    arrive(1)
    pick(1)
    weight_grads(False)
    finish(2)
    forward(3)
    arrive(2)
    pick(2)
    weight_grads(False)
    for which in range(2):
        keep(which).wait()
        for shift in range(1, PEERS):
            source = (e + PEERS - shift) % PEERS
            back(which, shift, source, source, source).wait_recv()
    outputs = returned[0].reshape(PEERS * capacity, width)
    grads = returned[1].reshape(PEERS * capacity, width)
    column = lax.broadcasted_iota(jnp.int32, (count, PEERS * capacity), 1).astype(jnp.float32)
    target = targets()
    total = jnp.zeros((count, width), jnp.float32)
    grad_total = jnp.zeros((count, width), jnp.float32)
    cotangent = all_ref[z, e, pl.ds(count, count), :].astype(jnp.float32)
    for choice in range(top):
        place = jnp.where(column == target[choice], 1.0, 0.0).astype(jnp.bfloat16)
        pair = dot(place, outputs, 0)
        total += gates_ref[:, choice : choice + 1] * pair
        grad_gates_ref[:, choice : choice + 1] = jnp.sum(cotangent * pair, axis=1, keepdims=True)
        grad_total += dot(place, grads, 0)
    out_ref[...] = total.astype(jnp.bfloat16)
    grad_tokens_ref[...] = grad_total.astype(jnp.bfloat16)
    finish(3)
    arrive(3)
    pick(3)
    weight_grads(False)
    for acc, ref in ((acc_gate, dw_gate_ref), (acc_up, dw_up_ref), (acc_down, dw_down_ref)):
        ref[...] = (acc[...] * (1.0 / REPS)).astype(jnp.bfloat16)
    for step in range(REPS):
        drain(step)
    for which in range(2):
        for shift in range(1, PEERS):
            peer = (e + shift) % PEERS
            back(which, shift, peer, e, peer).wait_send()


def store_kernel(*refs):
    half = len(refs) // 2
    copies = [pltpu.make_async_copy(refs[i], refs[half + i], refs[-1].at[i]) for i in range(half)]
    for copy in copies:
        copy.start()
    for copy in copies:
        copy.wait()


def local_dense(tokens, expert_ids, gate_weights, w_gate, w_up, w_down, grad_out):
    count, width = tokens.shape
    top = expert_ids.shape[1]
    units = w_gate.shape[1]
    share = units // REPS
    capacity = 2 * top * count // PEERS

    dma = pltpu.SemaphoreType.DMA
    vmem = pl.BlockSpec(memory_space=pltpu.VMEM)
    anywhere = pl.BlockSpec(memory_space=pl.ANY)
    bf16, f32 = jnp.bfloat16, jnp.float32
    slots = PEERS * capacity
    results = pl.pallas_call(
        moe_kernel,
        out_shape=[
            jax.ShapeDtypeStruct((count, width), bf16),
            jax.ShapeDtypeStruct((count, width), bf16),
            jax.ShapeDtypeStruct((count, top), f32),
            *[jax.ShapeDtypeStruct((share, width), bf16)] * 3,
        ],
        in_specs=[anywhere, anywhere, vmem, vmem, anywhere, anywhere, anywhere],
        out_specs=[vmem] * 6,
        scratch_shapes=[
            pltpu.VMEM((REPS, PEERS, 2 * count + EXTRA, width), bf16),
            *[pltpu.VMEM((units, width), bf16)] * 3,
            pltpu.VMEM((slots, width), bf16),
            pltpu.VMEM((slots, width), bf16),
            pltpu.VMEM((PEERS, count), f32),
            pltpu.VMEM((PEERS, count), f32),
            pltpu.VMEM((slots, width), f32),
            pltpu.VMEM((slots, width), f32),
            pltpu.VMEM((2, PEERS, capacity, width), bf16),
            pltpu.VMEM((2, PEERS, capacity, width), bf16),
            *[pltpu.VMEM((share, width), f32)] * 3,
            dma((2,)),
            dma((3,)),
            dma((2,)),
            dma((8, REPS)),
            dma((8, REPS)),
            dma((REPS,)),
            dma((REPS,)),
            dma((REPS,)),
            dma((3, REPS)),
            dma((3, REPS)),
            dma((3, REPS)),
            dma((2, PEERS)),
            dma((2, PEERS)),
        ],
        compiler_params=pltpu.CompilerParams(
            collective_id=0, has_side_effects=True, vmem_limit_bytes=60 * 1024 * 1024
        ),
    )(
        tokens, grad_out, expert_ids, gate_weights, w_gate[0], w_up[0], w_down[0],
    )
    out, grad_tokens, grad_gates, *grads = pl.pallas_call(
        store_kernel,
        out_shape=[jax.ShapeDtypeStruct(result.shape, result.dtype) for result in results],
        in_specs=[anywhere] * len(results),
        out_specs=[anywhere] * len(results),
        scratch_shapes=[dma((len(results),))],
    )(*results)
    return (out, grad_tokens, grad_gates, *[grad[None] for grad in grads])


def solution(mesh):
    in_specs = (
        P(("rep", "exp"), None),
        P(("rep", "exp"), None),
        P(("rep", "exp"), None),
        P("exp", None, None),
        P("exp", None, None),
        P("exp", None, None),
        P(("rep", "exp"), None),
    )
    out_specs = (
        P(("rep", "exp"), None),
        P(("rep", "exp"), None),
        P(("rep", "exp"), None),
        P("exp", "rep", None),
        P("exp", "rep", None),
        P("exp", "rep", None),
    )
    local = local_dense if (mesh.shape["rep"], mesh.shape["exp"]) == (REPS, PEERS) else local_general
    return jax.shard_map(local, mesh=mesh, in_specs=in_specs, out_specs=out_specs, check_vma=False)
```

```python
import jax
import jax.numpy as jnp
from jax import lax
from jax.experimental import pallas as pl
from jax.experimental.pallas import tpu as pltpu
from jax.sharding import PartitionSpec as P


def silu_parts(gate_pre):
    sigmoid_value = jax.nn.sigmoid(gate_pre)
    active = gate_pre * sigmoid_value
    slope_term = sigmoid_value * (1.0 + gate_pre * (1.0 - sigmoid_value))
    return (active, slope_term)


def place_pairs(expert_ids, experts, capacity):
    flat_ids = expert_ids.reshape(-1)
    onehot = (flat_ids[:, None] == jnp.arange(experts, dtype=jnp.int32)[None, :]).astype(jnp.int32)
    before = jnp.cumsum(onehot, axis=0) - onehot
    position = jnp.sum(before * onehot, axis=1)
    return flat_ids * capacity + position


def expert_forward(rows_in, w_gate, w_up, w_down):
    gate_pre = jnp.einsum("erd,efd->erf", rows_in, w_gate, preferred_element_type=jnp.float32)
    up_pre = jnp.einsum("erd,efd->erf", rows_in, w_up, preferred_element_type=jnp.float32)
    active, slope_term = silu_parts(gate_pre)
    hidden = (active * up_pre).astype(jnp.bfloat16)
    outputs = jnp.einsum("erf,efd->erd", hidden, w_down, preferred_element_type=jnp.float32).astype(
        jnp.bfloat16
    )
    return (up_pre, active, slope_term, hidden, outputs)


def expert_backward(rows_grad, up_pre, active, slope_term, w_gate, w_up, w_down):
    grad_hidden = jnp.einsum("erd,efd->erf", rows_grad, w_down, preferred_element_type=jnp.float32)
    grad_gate = (grad_hidden * up_pre * slope_term).astype(jnp.bfloat16)
    grad_up = (grad_hidden * active).astype(jnp.bfloat16)
    from_gate = jnp.einsum("erf,efd->erd", grad_gate, w_gate, preferred_element_type=jnp.float32)
    from_up = jnp.einsum("erf,efd->erd", grad_up, w_up, preferred_element_type=jnp.float32)
    grad_rows = (from_gate + from_up).astype(jnp.bfloat16)
    return (grad_gate, grad_up, grad_rows)


def local_general(tokens, expert_ids, gate_weights, w_gate, w_up, w_down, grad_out):
    local_tokens, model_width = tokens.shape
    top_count = expert_ids.shape[1]
    local_experts = w_gate.shape[0]
    peer_count = lax.axis_size("exp")
    replicas = lax.axis_size("rep")
    experts = local_experts * peer_count
    capacity = 2 * top_count * local_tokens // experts
    target = place_pairs(expert_ids, experts, capacity)
    pair_tokens = jnp.repeat(tokens, top_count, axis=0)
    pair_gates = gate_weights.reshape(-1)
    pair_grads = jnp.repeat(grad_out, top_count, axis=0).astype(jnp.float32)
    scaled_grads = (pair_gates[:, None] * pair_grads).astype(jnp.bfloat16)
    blank_rows = jnp.zeros((experts * capacity, model_width), jnp.bfloat16)
    token_buffer = blank_rows.at[target].set(pair_tokens).reshape(experts, capacity, model_width)
    grad_buffer = blank_rows.at[target].set(scaled_grads).reshape(experts, capacity, model_width)
    rows_in = lax.all_to_all(token_buffer, "exp", split_axis=0, concat_axis=1, tiled=True)
    up_pre, active, slope_term, hidden, outputs = expert_forward(rows_in, w_gate, w_up, w_down)
    returned = lax.all_to_all(outputs, "exp", split_axis=1, concat_axis=0, tiled=True)
    rows_grad = lax.all_to_all(grad_buffer, "exp", split_axis=0, concat_axis=1, tiled=True)
    grad_gate, grad_up, grad_rows = expert_backward(
        rows_grad, up_pre, active, slope_term, w_gate, w_up, w_down
    )
    returned_grads = lax.all_to_all(grad_rows, "exp", split_axis=1, concat_axis=0, tiled=True)
    pair_outputs = returned.reshape(experts * capacity, model_width)[target].astype(jnp.float32)
    pair_input_grads = returned_grads.reshape(experts * capacity, model_width)[target].astype(
        jnp.float32
    )
    weighted = (pair_gates[:, None] * pair_outputs).reshape(local_tokens, top_count, model_width)
    layer_output = jnp.sum(weighted, axis=1).astype(jnp.bfloat16)
    grad_gates = jnp.sum(pair_grads * pair_outputs, axis=1).reshape(local_tokens, top_count)
    grad_tokens = jnp.sum(
        pair_input_grads.reshape(local_tokens, top_count, model_width), axis=1
    ).astype(jnp.bfloat16)
    term_gate = jnp.einsum("erf,erd->fed", grad_gate, rows_in, preferred_element_type=jnp.float32)
    term_up = jnp.einsum("erf,erd->fed", grad_up, rows_in, preferred_element_type=jnp.float32)
    term_down = jnp.einsum("erf,erd->fed", hidden, rows_grad, preferred_element_type=jnp.float32)
    summed = lax.psum_scatter(
        jnp.concatenate([term_gate, term_up, term_down], axis=2).astype(jnp.bfloat16),
        "rep",
        scatter_dimension=0,
        tiled=True,
    ).astype(jnp.float32)
    summed = jnp.swapaxes(summed, 0, 1) / replicas
    grad_w_gate = summed[:, :, :model_width].astype(jnp.bfloat16)
    grad_w_up = summed[:, :, model_width : 2 * model_width].astype(jnp.bfloat16)
    grad_w_down = summed[:, :, 2 * model_width :].astype(jnp.bfloat16)
    return (layer_output, grad_tokens, grad_gates, grad_w_gate, grad_w_up, grad_w_down)


MESH = pl.DeviceIdType.MESH
REPS = 4
PEERS = 8
EXTRA = 16
RIDING = 96


def dot(a, b, b_dim):
    return lax.dot_general(a, b, (((1,), (b_dim,)), ((), ())), preferred_element_type=jnp.float32)


def moe_kernel(
    tokens_ref, grads_ref, ids_ref, gates_ref, w_gate_hbm, w_up_hbm, w_down_hbm,
    out_ref, grad_tokens_ref, grad_gates_ref, dw_gate_ref, dw_up_ref, dw_down_ref,
    all_ref, w_gate, w_up, w_down, rows_in, rows_grad, place_ref, gate_ref, out_acc, grad_acc, leaving, returned,
    acc_gate, acc_up, acc_down,
    load_sem, weight_sem, keep_sem, send_sem, recv_sem, zup_sem, zdown_sem, zrecv_sem,
    xup_sem, xdown_sem, xrecv_sem, back_send, back_recv,
):
    z = lax.axis_index("rep")
    e = lax.axis_index("exp")
    core, x, y = e % 2, (e // 2) % 2, e // 4
    sib, xn, yn = e + 1 - 2 * core, e + 2 - 4 * x, e + 4 - 8 * y
    diag = xn + yn - e
    count, width = tokens_ref.shape
    rows = all_ref.shape[2]
    capacity = leaving.shape[2]
    share = w_gate.shape[0] // REPS
    top = ids_ref.shape[0]
    cut = rows - RIDING
    riding = pl.ds(cut, RIDING)

    side = z // 2
    near = z + side * (3 - 2 * z)
    layers = [z]
    for step in range(1, REPS):
        mirrored = step - near if step == 1 else step
        layers.append(mirrored + side * (3 - 2 * mirrored))

    loads = [
        pltpu.make_async_copy(tokens_ref, all_ref.at[z, e, pl.ds(0, count)], load_sem.at[0]),
        pltpu.make_async_copy(grads_ref, all_ref.at[z, e, pl.ds(count, count)], load_sem.at[1]),
    ]
    weights = [
        pltpu.make_async_copy(w_gate_hbm, w_gate, weight_sem.at[0]),
        pltpu.make_async_copy(w_up_hbm, w_up, weight_sem.at[1]),
        pltpu.make_async_copy(w_down_hbm, w_down, weight_sem.at[2]),
    ]
    def pack_gates():
        line = lax.broadcasted_iota(jnp.int32, (PEERS, count), 0)
        value = jnp.zeros((PEERS, count), jnp.float32)
        for choice in range(top):
            value += jnp.where(line == ids_ref[choice : choice + 1, :], gates_ref[choice : choice + 1, :], 0.0)
        parts = []
        for _ in range(3):
            part = value.astype(jnp.bfloat16).astype(jnp.float32)
            parts.append(part)
            value = value - part
        row = lax.broadcasted_iota(jnp.int32, (EXTRA, count), 0)
        for expert in range(PEERS):
            tile = jnp.zeros((EXTRA, count), jnp.float32)
            for index, part in enumerate(parts):
                tile = jnp.where(row == index, part[expert : expert + 1, :], tile)
            lanes = pl.ds(expert * count, count)
            all_ref[z, e, pl.ds(2 * count, EXTRA), lanes] = tile.astype(jnp.bfloat16)

    def pair_columns():
        line = lax.broadcasted_iota(jnp.int32, (PEERS, count), 0)
        picks = [line == ids_ref[choice : choice + 1, :] for choice in range(top)]
        named = sum(jnp.where(picked, 1.0, 0.0) for picked in picks)
        row = lax.broadcasted_iota(jnp.int32, (count, count), 0)
        lane = lax.broadcasted_iota(jnp.int32, (count, count), 1)
        before = dot(named.astype(jnp.bfloat16), jnp.where(row < lane, 1.0, 0.0).astype(jnp.bfloat16), 0)
        slot = before + (line * capacity).astype(jnp.float32)
        table = jnp.zeros((count, count), jnp.float32)
        for choice, picked in enumerate(picks):
            target = jnp.sum(jnp.where(picked, slot, 0.0), axis=0, keepdims=True)
            table = jnp.where(row == choice, target, table)
            table = jnp.where(row == top + choice, gates_ref[choice : choice + 1, :], table)
        return table.T

    for copy in loads:
        copy.start()
    for copy in weights:
        copy.start()

    barrier = pltpu.get_barrier_semaphore()
    for shift in range(1, PEERS):
        peer = (e + shift) % PEERS
        pl.semaphore_signal(barrier, inc=1, device_id={"rep": z, "exp": peer}, device_id_type=MESH)

    @pl.when(z > 0)
    def _():
        pl.semaphore_signal(barrier, inc=1, device_id={"rep": z - 1, "exp": e}, device_id_type=MESH)

    @pl.when(z < REPS - 1)
    def _():
        pl.semaphore_signal(barrier, inc=1, device_id={"rep": z + 1, "exp": e}, device_id_type=MESH)

    pack_gates()
    inside = jnp.logical_and(z > 0, z < REPS - 1)

    @pl.when(inside)
    def _():
        pl.semaphore_wait(barrier, PEERS + 1)

    @pl.when(jnp.logical_not(inside))
    def _():
        pl.semaphore_wait(barrier, PEERS)

    def plane(kind, layer, owner, part, peer):
        block = all_ref.at[layer, owner] if part is None else all_ref.at[layer, owner, part]
        return pltpu.make_async_remote_copy(
            src_ref=block,
            dst_ref=block,
            send_sem=send_sem.at[kind, layer],
            recv_sem=recv_sem.at[kind, layer],
            device_id={"rep": z, "exp": peer},
            device_id_type=MESH,
        )

    def along(sem, layer, step):
        return pltpu.make_async_remote_copy(
            src_ref=all_ref.at[layer, e],
            dst_ref=all_ref.at[layer, e],
            send_sem=sem.at[layer],
            recv_sem=zrecv_sem.at[layer],
            device_id={"rep": z + step, "exp": e},
            device_id_type=MESH,
        )

    def spans(step):
        whole = rows if step == 0 else cut
        half = whole // 32 * 16
        return pl.ds(0, whole), pl.ds(0, half), pl.ds(half, whole - half)

    def direct(step):
        layer, (whole, _, _) = layers[step], spans(step)
        return [plane(0, layer, e, whole, xn), plane(1, layer, e, whole, yn), plane(2, layer, e, None, sib)]

    def relayed(step):
        layer, (_, first, second) = layers[step], spans(step)
        return [
            plane(3, layer, xn, first, yn),
            plane(5, layer, xn, None, sib),
            plane(4, layer, yn, second, xn),
            plane(6, layer, yn, None, sib),
        ]

    def pass_on(layer, action):
        @pl.when(jnp.logical_and(layer <= z, z < REPS - 1))
        def _():
            action(along(zup_sem, layer, 1))

        @pl.when(jnp.logical_and(layer >= z, z > 0))
        def _():
            action(along(zdown_sem, layer, -1))

    def rider(sem, index, layer, step):
        block = all_ref.at[layer, (xn, yn, diag)[index], riding]
        return pltpu.make_async_remote_copy(
            src_ref=block,
            dst_ref=block,
            send_sem=sem.at[index, layer],
            recv_sem=xrecv_sem.at[index, layer],
            device_id={"rep": z + step, "exp": e},
            device_id_type=MESH,
        )

    def pass_rider(index, layer, action):
        @pl.when(jnp.logical_and(layer <= z, z < REPS - 1))
        def _():
            action(rider(xup_sem, index, layer, 1))

        @pl.when(jnp.logical_and(layer >= z, z > 0))
        def _():
            action(rider(xdown_sem, index, layer, -1))

    def ride(step, index):
        layer = layers[step]
        if step:
            rider(xup_sem, index, layer, 0).wait_recv()
        pass_rider(index, layer, lambda copy: copy.start())

    def inject(step):
        layer = layers[step]
        if step:
            along(zup_sem, layer, 0).wait_recv()
        pass_on(layer, lambda copy: copy.start())
        for copy in direct(step):
            copy.start()

    def forward(step):
        layer, (whole, _, _) = layers[step], spans(step)
        copies = relayed(step)
        plane(0, layer, xn, whole, xn).wait_recv()
        copies[0].start()
        plane(1, layer, yn, whole, yn).wait_recv()
        copies[2].start()
        ride(step, 0)
        copies[1].start()
        ride(step, 1)
        copies[3].start()

    def finish(step):
        layer, (_, first, second) = layers[step], spans(step)
        plane(3, layer, diag, first, yn).wait_recv()
        plane(4, layer, diag, second, xn).wait_recv()
        ride(step, 2)
        plane(7, layer, diag, None, sib).start()

    def arrive(step):
        for kind in (2, 5, 6, 7):
            plane(kind, layers[step], sib, None, sib).wait_recv()

    def drain(step):
        layer = layers[step]
        for copy in direct(step) + relayed(step) + [plane(7, layer, diag, None, sib)]:
            copy.wait_send()
        pass_on(layer, lambda copy: copy.wait_send())
        for index in range(3):
            pass_rider(index, layer, lambda copy: copy.wait_send())

    def pick(step):
        layer = layers[step]
        lanes = pl.ds(pl.multiple_of(e * count, count), count)
        for block in range(PEERS):
            parts = all_ref[layer, block, pl.ds(2 * count, EXTRA), lanes].astype(jnp.float32)
            gate_ref[block : block + 1, :] = jnp.sum(parts, axis=0, keepdims=True)
        gates = gate_ref[...]
        used = jnp.where(gates > 0.0, 1.0, 0.0)
        earlier = lax.broadcasted_iota(jnp.int32, (count, count), 0)
        later = lax.broadcasted_iota(jnp.int32, (count, count), 1)
        before = jnp.where(earlier < later, 1.0, 0.0).astype(jnp.bfloat16)
        position = dot(used.astype(jnp.bfloat16), before, 0)
        place_ref[...] = jnp.where(gates > 0.0, position, -1.0)

        def body(block, carry):
            slot = lax.broadcasted_iota(jnp.int32, (capacity, count), 0).astype(jnp.float32)
            select = jnp.where(slot == place_ref[pl.ds(block, 1), :], 1.0, 0.0)
            slot_gates = jnp.sum(select * gate_ref[pl.ds(block, 1), :], axis=1, keepdims=True)
            select = select.astype(jnp.bfloat16)
            span = pl.ds(pl.multiple_of(block * capacity, capacity), capacity)
            rows_in[span, :] = dot(select, all_ref[layer, block, pl.ds(0, count), :], 0).astype(jnp.bfloat16)
            rows_grad[span, :] = (
                slot_gates * dot(select, all_ref[layer, block, pl.ds(count, count), :], 0)
            ).astype(jnp.bfloat16)
            return carry

        lax.fori_loop(0, PEERS, body, 0)

    def pointwise(gate_pre, up_pre, grad_hidden):
        sigmoid = 1.0 / (1.0 + jnp.exp(-gate_pre))
        active = gate_pre * sigmoid
        slope = sigmoid * (1.0 + gate_pre * (1.0 - sigmoid))
        hidden = (active * up_pre).astype(jnp.bfloat16)
        grad_gate = (grad_hidden * up_pre * slope).astype(jnp.bfloat16)
        grad_up = (grad_hidden * active).astype(jnp.bfloat16)
        return hidden, grad_gate, grad_up

    def own_rows(low, high):
        tile = rows_in.shape[0] // 2

        def body(index, carry):
            units = pl.ds(pl.multiple_of((index // 2) * share, share), share)
            span = pl.ds(pl.multiple_of((index % 2) * tile, tile), tile)
            gate, up, down = w_gate[units, :], w_up[units, :], w_down[units, :]
            row_in, row_grad = rows_in[span, :], rows_grad[span, :]
            hidden, grad_gate, grad_up = pointwise(dot(row_in, gate, 1), dot(row_in, up, 1), dot(row_grad, down, 1))
            out_acc[span, :] += dot(hidden, down, 0)
            grad_acc[span, :] += dot(grad_gate, gate, 0) + dot(grad_up, up, 0)
            return carry

        lax.fori_loop(low, high, body, 0)

    def weight_grads(start):
        units = pl.ds(pl.multiple_of(z * share, share), share)
        row_in, row_grad = rows_in[...], rows_grad[...]
        hidden, grad_gate, grad_up = pointwise(
            dot(w_gate[units, :], row_in, 1), dot(w_up[units, :], row_in, 1), dot(w_down[units, :], row_grad, 1)
        )
        for acc, lhs, rhs in ((acc_gate, grad_gate, row_in), (acc_up, grad_up, row_in), (acc_down, hidden, row_grad)):
            if start:
                acc[...] = dot(lhs, rhs, 0)
            else:
                acc[...] += dot(lhs, rhs, 0)

    def back(which, shift, source, slot, peer):
        return pltpu.make_async_remote_copy(
            src_ref=leaving.at[which, source],
            dst_ref=returned.at[which, slot],
            send_sem=back_send.at[which, shift],
            recv_sem=back_recv.at[which, shift],
            device_id={"rep": z, "exp": peer},
            device_id_type=MESH,
        )

    def keep(which):
        return pltpu.make_async_copy(leaving.at[which, e], returned.at[which, e], keep_sem.at[which])

    for copy in loads:
        copy.wait()
    inject(0)
    out_acc[...] = jnp.zeros_like(out_acc)
    grad_acc[...] = jnp.zeros_like(grad_acc)
    for copy in weights:
        copy.wait()
    inject(1)
    forward(0)
    inject(2)
    finish(0)
    forward(1)
    arrive(0)
    pick(0)
    own_rows(0, REPS)
    inject(3)
    finish(1)
    own_rows(REPS, 2 * REPS)
    for which, acc in ((0, out_acc), (1, grad_acc)):
        leaving[which] = acc[...].astype(jnp.bfloat16).reshape(leaving.shape[1:])
    for which in range(2):
        keep(which).start()
        for shift in range(1, PEERS):
            peer = (e + shift) % PEERS
            back(which, shift, peer, e, peer).start()
    forward(2)
    weight_grads(True)
    arrive(1)
    pick(1)
    weight_grads(False)
    finish(2)
    forward(3)
    arrive(2)
    pick(2)
    weight_grads(False)
    for which in range(2):
        keep(which).wait()
        for shift in range(1, PEERS):
            source = (e + PEERS - shift) % PEERS
            back(which, shift, source, source, source).wait_recv()
    outputs = returned[0].reshape(PEERS * capacity, width)
    grads = returned[1].reshape(PEERS * capacity, width)
    column = lax.broadcasted_iota(jnp.int32, (count, PEERS * capacity), 1).astype(jnp.float32)
    columns = pair_columns()
    lane = lax.broadcasted_iota(jnp.int32, (count, count), 1)
    table = jnp.zeros((count, count), jnp.float32)
    total = jnp.zeros((count, width), jnp.float32)
    grad_total = jnp.zeros((count, width), jnp.float32)
    cotangent = all_ref[z, e, pl.ds(count, count), :].astype(jnp.float32)
    for choice in range(top):
        place = jnp.where(column == columns[:, choice : choice + 1], 1.0, 0.0).astype(jnp.bfloat16)
        pair = dot(place, outputs, 0)
        total += columns[:, top + choice : top + choice + 1] * pair
        table = jnp.where(lane == choice, jnp.sum(cotangent * pair, axis=1, keepdims=True), table)
        grad_total += dot(place, grads, 0)
    grad_gates_ref[...] = table.T[:top, :]
    out_ref[...] = total.astype(jnp.bfloat16)
    grad_tokens_ref[...] = grad_total.astype(jnp.bfloat16)
    finish(3)
    arrive(3)
    pick(3)
    weight_grads(False)
    for acc, ref in ((acc_gate, dw_gate_ref), (acc_up, dw_up_ref), (acc_down, dw_down_ref)):
        ref[...] = (acc[...] * (1.0 / REPS)).astype(jnp.bfloat16)
    for step in range(REPS):
        drain(step)
    for which in range(2):
        for shift in range(1, PEERS):
            peer = (e + shift) % PEERS
            back(which, shift, peer, e, peer).wait_send()


def store_kernel(*refs):
    half = len(refs) // 2
    copies = [pltpu.make_async_copy(refs[i], refs[half + i], refs[-1].at[i]) for i in range(half)]
    for copy in copies:
        copy.start()
    for copy in copies:
        copy.wait()


def local_dense(tokens, expert_ids, gate_weights, w_gate, w_up, w_down, grad_out):
    count, width = tokens.shape
    top = expert_ids.shape[1]
    units = w_gate.shape[1]
    share = units // REPS
    capacity = 2 * top * count // PEERS

    dma = pltpu.SemaphoreType.DMA
    vmem = pl.BlockSpec(memory_space=pltpu.VMEM)
    anywhere = pl.BlockSpec(memory_space=pl.ANY)
    bf16, f32 = jnp.bfloat16, jnp.float32
    slots = PEERS * capacity
    results = pl.pallas_call(
        moe_kernel,
        out_shape=[
            jax.ShapeDtypeStruct((count, width), bf16),
            jax.ShapeDtypeStruct((count, width), bf16),
            jax.ShapeDtypeStruct((top, count), f32),
            *[jax.ShapeDtypeStruct((share, width), bf16)] * 3,
        ],
        in_specs=[anywhere, anywhere, vmem, vmem, anywhere, anywhere, anywhere],
        out_specs=[vmem] * 6,
        scratch_shapes=[
            pltpu.VMEM((REPS, PEERS, 2 * count + EXTRA, width), bf16),
            *[pltpu.VMEM((units, width), bf16)] * 3,
            pltpu.VMEM((slots, width), bf16),
            pltpu.VMEM((slots, width), bf16),
            pltpu.VMEM((PEERS, count), f32),
            pltpu.VMEM((PEERS, count), f32),
            pltpu.VMEM((slots, width), f32),
            pltpu.VMEM((slots, width), f32),
            pltpu.VMEM((2, PEERS, capacity, width), bf16),
            pltpu.VMEM((2, PEERS, capacity, width), bf16),
            *[pltpu.VMEM((share, width), f32)] * 3,
            dma((2,)),
            dma((3,)),
            dma((2,)),
            dma((8, REPS)),
            dma((8, REPS)),
            dma((REPS,)),
            dma((REPS,)),
            dma((REPS,)),
            dma((3, REPS)),
            dma((3, REPS)),
            dma((3, REPS)),
            dma((2, PEERS)),
            dma((2, PEERS)),
        ],
        compiler_params=pltpu.CompilerParams(
            collective_id=0, has_side_effects=True, vmem_limit_bytes=60 * 1024 * 1024
        ),
    )(
        tokens, grad_out, expert_ids.T, gate_weights.T, w_gate[0], w_up[0], w_down[0],
    )
    out, grad_tokens, grad_gates, *grads = pl.pallas_call(
        store_kernel,
        out_shape=[jax.ShapeDtypeStruct(result.shape, result.dtype) for result in results],
        in_specs=[vmem] * len(results),
        out_specs=[anywhere] * len(results),
        scratch_shapes=[dma((len(results),))],
    )(*results)
    return (out, grad_tokens, grad_gates.T, *[grad[None] for grad in grads])


def solution(mesh):
    in_specs = (
        P(("rep", "exp"), None),
        P(("rep", "exp"), None),
        P(("rep", "exp"), None),
        P("exp", None, None),
        P("exp", None, None),
        P("exp", None, None),
        P(("rep", "exp"), None),
    )
    out_specs = (
        P(("rep", "exp"), None),
        P(("rep", "exp"), None),
        P(("rep", "exp"), None),
        P("exp", "rep", None),
        P("exp", "rep", None),
        P("exp", "rep", None),
    )
    local = local_dense if (mesh.shape["rep"], mesh.shape["exp"]) == (REPS, PEERS) else local_general
    return jax.shard_map(local, mesh=mesh, in_specs=in_specs, out_specs=out_specs, check_vma=False)
```
